256 devices in a mesh: section: 16 (over y_hi, z), dp: 8 (over y_lo, x), mp: 2 (over core).
Axes of the slice: x: 4, y: 4 (y_hi: 2, y_lo: 2; y = y_hi * 2 + y_lo), z: 8, core: 2. Of those that a mesh axis runs over, the one named last changes fastest.
Arguments:
- old_w: float32 [16, 8, 16, 26, 3328], P(None, 'dp', 'section', None, 'mp'), may hold values from -0.109375 to 0.109375
- old_m: bfloat16 [16, 8, 16, 26, 3328], P(None, 'dp', 'section', None, 'mp'), may hold values from -12 to 12
- old_v: bfloat16 [16, 8, 16, 26, 3328], P(None, 'dp', 'section', None, 'mp'), may hold values from 0.5 to 20
- old_slot_layer: int32 [16], replicated, may hold values from 0 to 15, each once
- norm_gain: float32 [16, 3328], P('section'), may hold values from 0.5 to 2
- tokens: bfloat16 [8, 128, 3328], P(None, 'dp'), may hold values from -6 to 6
- cotangent: bfloat16 [8, 128, 3328], P(None, 'dp'), may hold values from -6 to 6
Outputs:
- new_w: float32 [16, 3328, 3328], P('section', 'dp', 'mp')
- new_m: bfloat16 [16, 3328, 3328], P('section', 'dp', 'mp')
- new_v: bfloat16 [16, 3328, 3328], P('section', 'dp', 'mp')
The draws below stay inside these ranges and needn't reach their ends.
Inputs may be any that keep to these rules, and one draw needn't show every extreme that they name: `old_slot_layer`: every layer number appears exactly once.
All inputs are finite; a program needn't handle non-finite values.
Results may differ from the reference program's by a relative error of at most 0.028.
Values may be sent and summed in bfloat16 or wider, within the bound.
A program may use at most 128 MiB of HBM per device.

```python
import math
import jax
import jax.numpy as jnp
from jax import lax

E = 3328
MB = 8
LAYERS = 16
PR = 26
TOKENS = 128
N_SECTION = 16
N_DP = 8


def block_scale(key, extent, cuts, least, high):
    level, own = 1.0, jax.random.fold_in(key, 6)
    for dim, parts in cuts:
        heights = jnp.exp(jax.random.uniform(jax.random.fold_in(own, dim), (parts,), jnp.float32, least / len(cuts), high / len(cuts)))
        level = level * jnp.repeat(heights, extent[dim] // parts).reshape([-1 if axis == dim else 1 for axis in range(len(extent))])
    return level


def centred(stream_key, shape, scale, reach, shards=(), held_as=jnp.bfloat16):
    gain = block_scale(stream_key, shape, shards, -0.22, 0.18) if shards else 1.0
    result = jax.random.normal(stream_key, shape, jnp.float32) * scale * gain
    return jnp.minimum(jnp.maximum(result, -reach), reach).astype(held_as)


def setup_inputs(seed: int = 0) -> dict:
    key_of = jax.random.split(jax.random.key(seed), 8)
    return {
        "old_w": centred(key_of[0], (LAYERS, N_DP, N_SECTION, PR, E), E ** -0.5, 0.109375, ((1, 8), (2, 16), (4, 2)), jnp.float32),
        "old_m": centred(key_of[1], (LAYERS, N_DP, N_SECTION, PR, E), 2.0, 12.0, ((1, 8), (2, 16), (4, 2))),
        "old_v": jnp.clip(jnp.exp(math.log(20.0) - 3.6888795 * jax.random.uniform(key_of[2], (LAYERS, N_DP, N_SECTION, PR, E), jnp.float32) ** block_scale(key_of[2], (LAYERS, N_DP, N_SECTION, PR, E), ((1, 8), (2, 16), (4, 2)), -0.2, 0.2)), 0.5, 20.0).astype(jnp.bfloat16),
        "old_slot_layer": jax.random.permutation(key_of[3], LAYERS).astype(jnp.int32),
        "norm_gain": jnp.clip(jnp.exp(math.log(2.0) - 1.3862944 * jax.random.uniform(key_of[4], (LAYERS, E), jnp.float32) ** block_scale(key_of[4], (LAYERS, E), ((0, 16),), -0.2, 0.2)), 0.5, 2.0),
        "tokens": centred(key_of[5], (MB, TOKENS, E), 1.0, 6.0, ((1, 8),)),
        "cotangent": centred(key_of[6], (MB, TOKENS, E), 1.0, 6.0, ((1, 8),)),
    }


eps_norm = 1e-05
beta_one = 0.9
beta_two = 0.95
learn_rate = 0.001
decay_rate = 0.1
adam_eps = 1e-08
step_count = 1000.0

def silu_slope(values):
    sigmoid_value = jax.nn.sigmoid(values)
    return sigmoid_value * (1.0 + values * (1.0 - sigmoid_value))

def row_scale_of(inputs):
    widened = inputs.astype(jnp.float32)
    return lax.rsqrt(lax.optimization_barrier(jnp.mean(widened * widened, axis=1, keepdims=True)) + eps_norm)

def reference(old_w, old_m, old_v, old_slot_layer, norm_gain, tokens, cotangent):
    layer_total = old_w.shape[0]
    full_width = old_w.shape[-1]
    layer_ids = jnp.arange(layer_total, dtype=jnp.int32)
    matches = (old_slot_layer[None, :] == layer_ids[:, None]).astype(jnp.int32)
    inverse = lax.optimization_barrier(jnp.sum(matches * layer_ids[None, :], axis=1)).astype(jnp.int32)
    master = jnp.take(old_w.reshape(layer_total, full_width, full_width), inverse, axis=0)
    first_moment = jnp.take(old_m.reshape(layer_total, full_width, full_width), inverse, axis=0)
    second_moment = jnp.take(old_v.reshape(layer_total, full_width, full_width), inverse, axis=0)
    current = tokens.reshape(-1, full_width)
    stashed = []
    normed_list = []
    preact_list = []
    for layer in range(layer_total):
        weight_copy = master[layer].astype(jnp.bfloat16)
        widened = current.astype(jnp.float32)
        row_scale = row_scale_of(current)
        normed = (widened * row_scale * norm_gain[layer]).astype(jnp.bfloat16)
        preact = jnp.dot(normed, weight_copy, preferred_element_type=jnp.float32)
        stashed.append(current)
        normed_list.append(normed)
        preact_list.append(preact)
        current = (widened + jax.nn.silu(preact)).astype(jnp.bfloat16)
    back_grad = cotangent.reshape(-1, full_width)
    weights_out = []
    firsts_out = []
    seconds_out = []
    for layer in range(layer_total - 1, -1, -1):
        weight_copy = master[layer].astype(jnp.bfloat16)
        dpre = (back_grad.astype(jnp.float32) * silu_slope(preact_list[layer])).astype(jnp.bfloat16)
        weight_grad = jnp.dot(normed_list[layer].T, dpre, preferred_element_type=jnp.float32)
        dnormed = lax.dot_general(dpre, weight_copy, (((1,), (1,)), ((), ())), preferred_element_type=jnp.float32)
        inputs = stashed[layer]
        widened = inputs.astype(jnp.float32)
        row_scale = row_scale_of(inputs)
        weighted = norm_gain[layer] * dnormed
        row_stat = lax.optimization_barrier(jnp.mean(widened * weighted, axis=1, keepdims=True))
        cube = row_scale * row_scale * row_scale
        back_grad = (back_grad.astype(jnp.float32) + row_scale * weighted - widened * cube * row_stat).astype(jnp.bfloat16)
        moment_next = beta_one * first_moment[layer].astype(jnp.float32) + (1.0 - beta_one) * weight_grad
        second_next = beta_two * second_moment[layer].astype(jnp.float32) + (1.0 - beta_two) * weight_grad * weight_grad
        fix_one = 1.0 - beta_one ** step_count
        fix_two = 1.0 - beta_two ** step_count
        direction = moment_next / fix_one / (jnp.sqrt(second_next / fix_two) + adam_eps)
        weights_out.append(master[layer] - learn_rate * (direction + decay_rate * master[layer]))
        firsts_out.append(moment_next.astype(jnp.bfloat16))
        seconds_out.append(second_next.astype(jnp.bfloat16))
    new_w = jnp.stack(weights_out[::-1], axis=0)
    new_m = jnp.stack(firsts_out[::-1], axis=0)
    new_v = jnp.stack(seconds_out[::-1], axis=0)
    return (new_w, new_m, new_v)
```

```python
import functools

import jax
import jax.numpy as jnp
from jax import lax
from jax.experimental import pallas as pl
from jax.experimental.pallas import tpu as pltpu
from jax.sharding import PartitionSpec as P

eps_norm = 1e-05
beta_one = 0.9
beta_two = 0.95
learn_rate = 0.001
decay_rate = 0.1
adam_eps = 1e-08
step_count = 1000.0

MESH = pl.DeviceIdType.MESH
F32 = jnp.float32
BF16 = jnp.bfloat16
XS = 4


def remote(src, dst, send_sem, recv_sem, device):
    return pltpu.make_async_remote_copy(
        src_ref=src,
        dst_ref=dst,
        send_sem=send_sem,
        recv_sem=recv_sem,
        device_id=device,
        device_id_type=MESH,
    )


def relay_plan(rows):
    two_thirds = max(16, (rows * 2 // 3 + 15) // 16 * 16)
    half = (rows // 2 + 15) // 16 * 16
    return two_thirds, half


def kernel(
    sizes,
    order,
    old_w,
    old_m,
    old_v,
    gain,
    tokens,
    cotangent,
    new_w,
    new_m,
    new_v,
    w_send,
    m_send,
    v_send,
    w_recv,
    m_recv,
    v_recv,
    wide,
    block,
    weights,
    acts,
    outs,
    preacts,
    scales,
    normed,
    normed_t,
    feats,
    grads_in,
    grads_out,
    dpres,
    part_send,
    part_recv,
    stat_send,
    stat_recv,
    ws,
    wr,
    ms,
    mr,
    vs,
    vr,
    gs,
    gr,
    fs,
    fr,
    rs,
    rr,
    ps,
    pr,
    ss,
    sr,
    bs,
    br,
    ts,
    tr,
    ds,
    dr,
    local_sem,
):
    S, D, pr_rows, H, MB, R = sizes
    RB = S * pr_rows
    TOK = MB * R
    E = 2 * H
    s = lax.axis_index("section")
    a = lax.axis_index("dp")
    c = lax.axis_index("mp")
    sib = {"mp": 1 - c}

    barrier = pltpu.get_barrier_semaphore()

    @pl.loop(1, S)
    def _(k):
        pl.semaphore_signal(
            barrier, inc=1, device_id={"section": lax.rem(s + k, S)}, device_id_type=MESH
        )

    @pl.loop(1, D)
    def _(k):
        pl.semaphore_signal(
            barrier, inc=1, device_id={"dp": lax.rem(a + k, D)}, device_id_type=MESH
        )

    pl.semaphore_signal(barrier, inc=1, device_id=sib, device_id_type=MESH)

    @pl.when(s == 0)
    def _():
        @pl.loop(0, MB)
        def _(b):
            pltpu.make_async_copy(
                tokens.at[b, :, pl.ds(pl.multiple_of(c * H, 128), H)],
                acts.at[b, c],
                local_sem.at[b],
            ).start()

    @pl.when(s == S - 1)
    def _():
        @pl.loop(0, MB)
        def _(b):
            pltpu.make_async_copy(
                cotangent.at[b, :, pl.ds(pl.multiple_of(c * H, 128), H)],
                grads_in.at[b],
                local_sem.at[MB + b],
            ).start()

    @pl.loop(0, S)
    def _(k):
        w_send[k] = old_w[order[k]].astype(BF16)

    @pl.loop(0, S)
    def _(k):
        m_send[k] = old_m[order[k]]
        v_send[k] = old_v[order[k]]

    pl.semaphore_wait(barrier, S + D - 1)

    def scatter(send, recv, send_sems, recv_sems):
        @pl.loop(1, S)
        def _(k):
            to = lax.rem(s + k, S)
            remote(
                send.at[to], recv.at[s], send_sems.at[to], recv_sems.at[s], {"section": to}
            ).start()

        recv[s] = send[s]

    def arrived(send, recv, send_sems, recv_sems):
        @pl.loop(1, S)
        def _(k):
            of = lax.rem(s + k, S)
            remote(
                send.at[of], recv.at[of], send_sems.at[of], recv_sems.at[of], {"section": of}
            ).wait_recv()

    def drained(send, recv, send_sems, recv_sems):
        @pl.loop(1, S)
        def _(k):
            of = lax.rem(s + k, S)
            remote(
                send.at[of], recv.at[of], send_sems.at[of], recv_sems.at[of], {"section": of}
            ).wait_send()

    def assemble(recv, dst):
        @pl.loop(0, H // 128)
        def _(j):
            cols = pl.ds(pl.multiple_of(j * 128, 128), 128)
            for b in range(S):
                wide[pr_rows * b : pr_rows * (b + 1), :] = recv[b, :, cols].astype(F32)
            dst[:, cols] = wide[...].astype(BF16)

    scatter(w_send, w_recv, ws, wr)
    arrived(w_send, w_recv, ws, wr)
    scatter(m_send, m_recv, ms, mr)
    scatter(v_send, v_recv, vs, vr)
    assemble(w_recv, block)

    def rows_of(owner, r0, n):
        return weights.at[pl.ds(pl.multiple_of(owner * RB + r0, 16), n), :]

    own_copy = pltpu.make_async_copy(block, rows_of(a, 0, RB), local_sem.at[2 * MB])
    own_copy.start()
    pending = []
    if D == 2 * XS:
        x = lax.rem(a, XS)
        h = a // XS

        def at(dx, dh):
            hh = (1 - h) if dh else h
            return hh * XS + lax.rem(x + dx + XS, XS)

        third, half = relay_plan(RB)
        UP, DOWN, ACROSS = at(1, 0), at(-1, 0), at(0, 1)

        def start(sem, src, owner, r0, n, to):
            cp = remote(
                src, rows_of(owner, r0, n), gs.at[sem], gr.at[sem], {"dp": to}
            )
            cp.start()
            pending.append(cp)

        def relay(sem, owner, r0, n, to):
            start(sem, rows_of(owner, r0, n), owner, r0, n, to)

        def landed(sem, owner, r0, n):
            pltpu.make_async_copy(
                rows_of(owner, r0, n), rows_of(owner, r0, n), gr.at[sem]
            ).wait()

        def blk(r0, n):
            return block.at[pl.ds(r0, n), :]

        start(0, blk(third, RB - third), a, third, RB - third, ACROSS)
        start(1, blk(0, third), a, 0, third, ACROSS)
        start(2, blk(0, half), a, 0, half, UP)
        start(3, blk(half, RB - half), a, half, RB - half, DOWN)
        start(4, blk(half, RB - half), a, half, RB - half, UP)
        start(5, blk(0, half), a, 0, half, DOWN)
        landed(0, ACROSS, third, RB - third)
        relay(6, ACROSS, third, RB - third, UP)
        relay(7, ACROSS, third, RB - third, DOWN)
        landed(2, DOWN, 0, half)
        relay(8, DOWN, 0, half, UP)
        landed(3, UP, half, RB - half)
        relay(9, UP, half, RB - half, DOWN)
        landed(4, DOWN, half, RB - half)
        landed(5, UP, 0, half)
        relay(10, DOWN, 0, third, ACROSS)
        relay(11, UP, 0, third, ACROSS)
        landed(1, ACROSS, 0, third)
        landed(6, at(-1, 1), third, RB - third)
        landed(7, at(1, 1), third, RB - third)
        landed(10, at(-1, 1), 0, third)
        relay(12, at(-1, 1), 0, half, UP)
        landed(11, at(1, 1), 0, third)
        relay(13, at(1, 1), half, RB - half, DOWN)
        landed(8, at(2, 0), 0, half)
        landed(9, at(2, 0), half, RB - half)
        landed(12, at(2, 1), 0, half)
        landed(13, at(2, 1), half, RB - half)
    else:
        for k in range(1, D):
            to = lax.rem(a + k, D)
            cp = remote(block, rows_of(a, 0, RB), gs.at[k], gr.at[k], {"dp": to})
            cp.start()
            pending.append(cp)
        for k in range(1, D):
            of = lax.rem(a - k + D, D)
            pltpu.make_async_copy(rows_of(of, 0, RB), rows_of(of, 0, RB), gr.at[k]).wait()
    own_copy.wait()

    own_rows = pl.ds(pl.multiple_of(c * H, 128), H)
    sib_rows = pl.ds(pl.multiple_of((1 - c) * H, 128), H)
    gain_own = gain[c]
    gain_sib = gain[1 - c]

    @pl.loop(0, MB)
    def _(b):
        @pl.when(s == 0)
        def _():
            pltpu.make_async_copy(
                tokens.at[b, :, pl.ds(pl.multiple_of(c * H, 128), H)],
                acts.at[b, c],
                local_sem.at[b],
            ).wait()

        @pl.when(s > 0)
        def _():
            pltpu.make_async_copy(outs.at[b], acts.at[b, c], fr.at[b]).wait()

        remote(acts.at[b, c], acts.at[b, c], rs.at[b], rr.at[b], sib).start()
        x_own = acts[b, c].astype(F32)
        square = jnp.sum(x_own * x_own, axis=1, keepdims=True)
        total = jnp.dot(
            (x_own * gain_own).astype(BF16), weights[own_rows, :], preferred_element_type=F32
        )
        pltpu.make_async_copy(acts.at[b, 1 - c], acts.at[b, 1 - c], rr.at[b]).wait()
        x_sib = acts[b, 1 - c].astype(F32)
        square = square + jnp.sum(x_sib * x_sib, axis=1, keepdims=True)
        total = total + jnp.dot(
            (x_sib * gain_sib).astype(BF16), weights[sib_rows, :], preferred_element_type=F32
        )
        scale = lax.rsqrt(square * (1.0 / E) + eps_norm)
        pre = total * scale
        outs[b] = (x_own + jax.nn.silu(pre)).astype(BF16)

        @pl.when(s < S - 1)
        def _():
            remote(
                outs.at[b],
                acts.at[b, c],
                fs.at[b],
                fr.at[b],
                {"section": lax.rem(s + 1, S)},
            ).start()

        preacts[b] = pre
        scales[b] = jnp.broadcast_to(scale, (R, 128))
        rows = pl.ds(pl.multiple_of(b * R, R), R)
        normed[c, rows, :] = (x_own * scale * gain_own).astype(BF16)
        normed[1 - c, rows, :] = (x_sib * scale * gain_sib).astype(BF16)

    def features():
        for half_index in range(2):

            @pl.loop(0, H // 128)
            def _(j):
                cols = pl.ds(pl.multiple_of(j * 128, 128), 128)
                flipped = jnp.transpose(normed[half_index, :, cols].astype(F32))
                normed_t[pl.ds(pl.multiple_of(half_index * H + j * 128, 128), 128), :] = (
                    flipped.astype(BF16)
                )

        @pl.loop(1, D)
        def _(k):
            to = lax.rem(a + k, D)
            remote(
                normed_t.at[pl.ds(pl.multiple_of(to * RB, 16), RB), :],
                feats.at[:, pl.ds(pl.multiple_of(a * TOK, 128), TOK)],
                ts.at[to],
                tr.at[a],
                {"dp": to},
            ).start()

        feats[:, pl.ds(pl.multiple_of(a * TOK, 128), TOK)] = normed_t[
            pl.ds(pl.multiple_of(a * RB, 16), RB), :
        ]

    @pl.when(s < (S + 1) // 2)
    def _():
        features()

    def dpre_rows(owner, b):
        return dpres.at[pl.ds(pl.multiple_of(owner * TOK + b * R, R), R), :]

    @pl.loop(0, MB)
    def _(b):
        @pl.when(s == S - 1)
        def _():
            pltpu.make_async_copy(
                cotangent.at[b, :, pl.ds(pl.multiple_of(c * H, 128), H)],
                grads_in.at[b],
                local_sem.at[MB + b],
            ).wait()

        @pl.when(s < S - 1)
        def _():
            pltpu.make_async_copy(grads_out.at[b], grads_in.at[b], br.at[b]).wait()

        upstream = grads_in[b].astype(F32)
        pre = preacts[b]
        sig = jax.nn.sigmoid(pre)
        dpre = (upstream * (sig * (1.0 + pre * (1.0 - sig)))).astype(BF16)
        dpres[pl.ds(pl.multiple_of(a * TOK + b * R, R), R), :] = dpre

        @pl.when(s > 0)
        def _():
            stat = jnp.sum(dpre.astype(F32) * pre, axis=1, keepdims=True)
            stat_send[b] = jnp.broadcast_to(stat, (R, 128))
            remote(stat_send.at[b], stat_recv.at[b], ss.at[b], sr.at[b], sib).start()
            part_send[b] = lax.dot_general(
                dpre,
                weights[sib_rows, :],
                (((1,), (1,)), ((), ())),
                preferred_element_type=F32,
            ).astype(BF16)
            remote(part_send.at[b], part_recv.at[b], ps.at[b], pr.at[b], sib).start()
            part = lax.dot_general(
                dpre,
                weights[own_rows, :],
                (((1,), (1,)), ((), ())),
                preferred_element_type=F32,
            )
            pltpu.make_async_copy(stat_send.at[b], stat_recv.at[b], sr.at[b]).wait()
            scale = scales[b][:, :1]
            both = (stat + stat_recv[b][:, :1]) * (1.0 / E)
            pltpu.make_async_copy(part_send.at[b], part_recv.at[b], pr.at[b]).wait()
            dnormed = part + part_recv[b].astype(F32)
            back = (
                upstream
                + scale * (gain_own * dnormed)
                - acts[b, c].astype(F32) * (scale * scale * both)
            )
            grads_out[b] = back.astype(BF16)
            remote(
                grads_out.at[b],
                grads_in.at[b],
                bs.at[b],
                br.at[b],
                {"section": lax.rem(s + S - 1, S)},
            ).start()

        @pl.loop(1, D)
        def _(k):
            to = lax.rem(a + k, D)
            remote(
                dpre_rows(a, b), dpre_rows(a, b), ds.at[b, to], dr.at[b, a], {"dp": to}
            ).start()

    @pl.when(s >= (S + 1) // 2)
    def _():
        features()

    arrived(m_send, m_recv, ms, mr)
    assemble(m_recv, new_m.at[0])
    arrived(v_send, v_recv, vs, vr)
    assemble(v_recv, new_v.at[0])

    @pl.loop(1, D)
    def _(k):
        of = lax.rem(a + k, D)
        there = feats.at[:, pl.ds(pl.multiple_of(of * TOK, 128), TOK)]
        pltpu.make_async_copy(there, there, tr.at[of]).wait()

        @pl.loop(0, MB)
        def _(b):
            pltpu.make_async_copy(dpre_rows(of, b), dpre_rows(of, b), dr.at[b, of]).wait()

    fix_one = 1.0 - beta_one**step_count
    fix_two = 1.0 - beta_two**step_count

    def update(cols):
        grad = jnp.dot(feats[...], dpres[:, cols], preferred_element_type=F32)
        moment = beta_one * new_m[0, :, cols].astype(F32) + (1.0 - beta_one) * grad
        second = beta_two * new_v[0, :, cols].astype(F32) + (1.0 - beta_two) * grad * grad
        direction = moment / fix_one / (jnp.sqrt(second / fix_two) + adam_eps)
        master = block[:, cols].astype(F32)
        new_w[0, :, cols] = master - learn_rate * (direction + decay_rate * master)
        new_m[0, :, cols] = moment.astype(BF16)
        new_v[0, :, cols] = second.astype(BF16)

    @pl.loop(0, H // 256)
    def _(j):
        update(pl.ds(pl.multiple_of(j * 256, 128), 256))

    if H % 256:
        update(pl.ds(H - H % 256, H % 256))

    drained(w_send, w_recv, ws, wr)
    drained(m_send, m_recv, ms, mr)
    drained(v_send, v_recv, vs, vr)
    for cp in pending:
        cp.wait_send()

    @pl.loop(0, MB)
    def _(b):
        remote(acts.at[b, c], acts.at[b, c], rs.at[b], rr.at[b], sib).wait_send()

        @pl.when(s < S - 1)
        def _():
            remote(outs.at[b], acts.at[b, c], fs.at[b], fr.at[b], sib).wait_send()

        @pl.when(s > 0)
        def _():
            remote(stat_send.at[b], stat_recv.at[b], ss.at[b], sr.at[b], sib).wait_send()
            remote(part_send.at[b], part_recv.at[b], ps.at[b], pr.at[b], sib).wait_send()
            remote(grads_out.at[b], grads_in.at[b], bs.at[b], br.at[b], sib).wait_send()

        @pl.loop(1, D)
        def _(k):
            to = lax.rem(a + k, D)
            remote(
                dpre_rows(a, b), dpre_rows(a, b), ds.at[b, to], dr.at[b, a], {"dp": to}
            ).wait_send()

    @pl.loop(1, D)
    def _(k):
        to = lax.rem(a + k, D)
        remote(
            normed_t.at[pl.ds(pl.multiple_of(to * RB, 16), RB), :],
            feats.at[:, pl.ds(pl.multiple_of(a * TOK, 128), TOK)],
            ts.at[to],
            tr.at[a],
            {"dp": to},
        ).wait_send()


def local(old_w, old_m, old_v, old_slot_layer, norm_gain, tokens, cotangent):
    S = lax.axis_size("section")
    D = lax.axis_size("dp")
    PR, H = old_w.shape[3], old_w.shape[4]
    MB, R = tokens.shape[0], tokens.shape[1]
    RB = S * PR
    TOK = MB * R
    E = 2 * H
    layer_ids = jnp.arange(S, dtype=jnp.int32)
    matches = (old_slot_layer[None, :] == layer_ids[:, None]).astype(jnp.int32)
    order = jnp.sum(matches * layer_ids[None, :], axis=1)
    vmem = pl.BlockSpec(memory_space=pltpu.VMEM)
    anyspace = pl.BlockSpec(memory_space=pl.ANY)
    dma = pltpu.SemaphoreType.DMA
    new_w, new_m, new_v = pl.pallas_call(
        functools.partial(kernel, (S, D, PR, H, MB, R)),
        out_shape=(
            jax.ShapeDtypeStruct((1, RB, H), F32),
            jax.ShapeDtypeStruct((1, RB, H), BF16),
            jax.ShapeDtypeStruct((1, RB, H), BF16),
        ),
        in_specs=[pl.BlockSpec(memory_space=pltpu.SMEM), vmem, vmem, vmem, vmem, anyspace, anyspace],
        out_specs=(vmem, vmem, vmem),
        scratch_shapes=[
            pltpu.VMEM((S, PR, H), BF16),
            pltpu.VMEM((S, PR, H), BF16),
            pltpu.VMEM((S, PR, H), BF16),
            pltpu.VMEM((S, PR, H), BF16),
            pltpu.VMEM((S, PR, H), BF16),
            pltpu.VMEM((S, PR, H), BF16),
            pltpu.VMEM((RB, 128), F32),
            pltpu.VMEM((RB, H), BF16),
            pltpu.VMEM((E, H), BF16),
            pltpu.VMEM((MB, 2, R, H), BF16),
            pltpu.VMEM((MB, R, H), BF16),
            pltpu.VMEM((MB, R, H), F32),
            pltpu.VMEM((MB, R, 128), F32),
            pltpu.VMEM((2, TOK, H), BF16),
            pltpu.VMEM((E, TOK), BF16),
            pltpu.VMEM((RB, D * TOK), BF16),
            pltpu.VMEM((MB, R, H), BF16),
            pltpu.VMEM((MB, R, H), BF16),
            pltpu.VMEM((D * TOK, H), BF16),
            pltpu.VMEM((MB, R, H), BF16),
            pltpu.VMEM((MB, R, H), BF16),
            pltpu.VMEM((MB, R, 128), F32),
            pltpu.VMEM((MB, R, 128), F32),
            dma((S,)),
            dma((S,)),
            dma((S,)),
            dma((S,)),
            dma((S,)),
            dma((S,)),
            dma((14,)),
            dma((14,)),
            dma((MB,)),
            dma((MB,)),
            dma((MB,)),
            dma((MB,)),
            dma((MB,)),
            dma((MB,)),
            dma((MB,)),
            dma((MB,)),
            dma((MB,)),
            dma((MB,)),
            dma((D,)),
            dma((D,)),
            dma((MB, D)),
            dma((MB, D)),
            dma((2 * MB + 1,)),
        ],
        compiler_params=pltpu.CompilerParams(
            collective_id=0, has_side_effects=True, vmem_limit_bytes=63_000_000
        ),
    )(
        order,
        old_w.reshape(S, PR, H),
        old_m.reshape(S, PR, H),
        old_v.reshape(S, PR, H),
        norm_gain.reshape(2, 1, H),
        tokens,
        cotangent,
    )
    return new_w, new_m, new_v


def solution(mesh):
    placed = (
        P(None, "dp", "section", None, "mp"),
        P(None, "dp", "section", None, "mp"),
        P(None, "dp", "section", None, "mp"),
        P(),
        P("section", None),
        P(None, "dp", None),
        P(None, "dp", None),
    )
    return jax.shard_map(
        local,
        mesh=mesh,
        in_specs=placed,
        out_specs=(P("section", "dp", "mp"), P("section", "dp", "mp"), P("section", "dp", "mp")),
        check_vma=False,
    )
```

```python
import functools

import jax
import jax.numpy as jnp
from jax import lax
from jax.experimental import pallas as pl
from jax.experimental.pallas import tpu as pltpu
from jax.sharding import PartitionSpec as P

eps_norm = 1e-05
beta_one = 0.9
beta_two = 0.95
learn_rate = 0.001
decay_rate = 0.1
adam_eps = 1e-08
step_count = 1000.0

MESH = pl.DeviceIdType.MESH
F32 = jnp.float32
BF16 = jnp.bfloat16
XS = 4


def remote(src, dst, send_sem, recv_sem, device):
    return pltpu.make_async_remote_copy(
        src_ref=src,
        dst_ref=dst,
        send_sem=send_sem,
        recv_sem=recv_sem,
        device_id=device,
        device_id_type=MESH,
    )


def relay_plan(rows):
    two_thirds = max(16, (rows * 2 // 3 + 15) // 16 * 16)
    half = (rows // 2 + 15) // 16 * 16
    return two_thirds, half


def feature_width(rows, half):
    return max(
        -(-(rows * k % 128 + rows) // 128) * 128 for k in range(half // rows)
    )


def kernel(
    sizes,
    order,
    old_w,
    old_m,
    old_v,
    gain,
    tokens,
    cotangent,
    grad_out,
    block_out,
    m_out,
    v_out,
    w_send,
    m_send,
    v_send,
    w_recv,
    m_recv,
    v_recv,
    pick,
    wide,
    block,
    first,
    second,
    weights,
    flipped,
    acts,
    outs,
    preacts,
    scales,
    normed,
    raw_feats,
    feats,
    grads_in,
    grads_out,
    dpres,
    part_send,
    part_recv,
    stat_send,
    stat_recv,
    ws,
    wr,
    ms,
    mr,
    vs,
    vr,
    gs,
    gr,
    fs,
    fr,
    rs,
    rr,
    ps,
    pr,
    ss,
    sr,
    bs,
    br,
    ts,
    tr,
    ds,
    dr,
    local_sem,
    out_sem,
):
    S, D, pr_rows, H, MB, R = sizes
    RB = S * pr_rows
    TOK = MB * R
    E = 2 * H
    s = lax.axis_index("section")
    a = lax.axis_index("dp")
    c = lax.axis_index("mp")
    sib = {"mp": 1 - c}
    lanes = H // 128
    cut = (lanes + 1) // 2 * 128
    chunks = ((0, cut), (cut, H - cut))
    width = feature_width(RB, H)

    barrier = pltpu.get_barrier_semaphore()

    @pl.loop(1, S)
    def _(k):
        pl.semaphore_signal(
            barrier, inc=1, device_id={"section": lax.rem(s + k, S)}, device_id_type=MESH
        )

    @pl.loop(1, D)
    def _(k):
        pl.semaphore_signal(
            barrier, inc=1, device_id={"dp": lax.rem(a + k, D)}, device_id_type=MESH
        )

    pl.semaphore_signal(barrier, inc=1, device_id=sib, device_id_type=MESH)

    @pl.when(s == 0)
    def _():
        @pl.loop(0, MB)
        def _(b):
            pltpu.make_async_copy(
                tokens.at[b, :, pl.ds(pl.multiple_of(c * H, 128), H)],
                acts.at[b, c],
                local_sem.at[b],
            ).start()

    @pl.when(s == S - 1)
    def _():
        @pl.loop(0, MB)
        def _(b):
            pltpu.make_async_copy(
                cotangent.at[b, :, pl.ds(pl.multiple_of(c * H, 128), H)],
                grads_in.at[b],
                local_sem.at[MB + b],
            ).start()

    @pl.loop(0, S)
    def _(k):
        base = order[k] * (pr_rows * lanes)
        for j in range(lanes):
            w_send[k, :, 128 * j : 128 * (j + 1)] = old_w[
                pl.ds(base + j, pr_rows, stride=lanes), :
            ].astype(BF16)

    pl.semaphore_wait(barrier, S + D - 1)

    def send_piece(send, recv, send_sems, recv_sems, to):
        @pl.when(to != s)
        def _():
            remote(
                send.at[to], recv.at[s], send_sems.at[to], recv_sems.at[s], {"section": to}
            ).start()

    def arrived(send, recv, send_sems, recv_sems):
        @pl.loop(1, S)
        def _(k):
            of = lax.rem(s + k, S)
            remote(
                send.at[of], recv.at[of], send_sems.at[of], recv_sems.at[of], {"section": of}
            ).wait_recv()

    def drained(send, recv, send_sems, recv_sems):
        @pl.loop(1, S)
        def _(k):
            of = lax.rem(s + k, S)
            remote(
                send.at[of], recv.at[of], send_sems.at[of], recv_sems.at[of], {"section": of}
            ).wait_send()

    def assemble(recv, dst):
        @pl.loop(0, H // 128)
        def _(j):
            cols = pl.ds(pl.multiple_of(j * 128, 128), 128)
            for b in range(S):
                wide[pr_rows * b : pr_rows * (b + 1), :] = recv[b, 0:pr_rows, cols].astype(F32)
            dst[:, cols] = wide[...].astype(BF16)

    @pl.loop(0, S)
    def _(to):
        send_piece(w_send, w_recv, ws, wr, to)

    w_recv[s] = w_send[s]
    arrived(w_send, w_recv, ws, wr)
    assemble(w_recv, block)

    def rows_of(owner, r0, n):
        return weights.at[pl.ds(pl.multiple_of(owner * RB + r0, 16), n), :]

    def prepare():
        padded = m_send.shape[1]

        @pl.loop(0, S)
        def _(k):
            shape = (padded, pr_rows * S)
            row = lax.broadcasted_iota(jnp.int32, shape, 0)
            col = lax.broadcasted_iota(jnp.int32, shape, 1)
            hit = col == row * S + order[k]
            pick[pl.ds(pl.multiple_of(k * padded, 16), padded), :] = jnp.where(
                hit & (row < pr_rows), 1.0, 0.0
            ).astype(BF16)

        def select(old, send):
            @pl.loop(0, lanes)
            def _(j):
                cols = pl.ds(pl.multiple_of(j * 128, 128), 128)
                flat = old[:, :, cols].reshape(pr_rows * S, 128)
                send[:, :, cols] = (
                    jnp.dot(pick[...], flat, preferred_element_type=F32)
                    .astype(BF16)
                    .reshape(S, padded, 128)
                )

        select(old_m, m_send)
        select(old_v, v_send)
        m_recv[s] = m_send[s]
        v_recv[s] = v_send[s]

    own_copy = pltpu.make_async_copy(block, rows_of(a, 0, RB), local_sem.at[2 * MB])
    own_copy.start()
    pending = []
    if D == 2 * XS:
        x = lax.rem(a, XS)
        h = a // XS

        def at(dx, dh):
            hh = (1 - h) if dh else h
            return hh * XS + lax.rem(x + dx + XS, XS)

        third, half = relay_plan(RB)
        UP, DOWN, ACROSS = at(1, 0), at(-1, 0), at(0, 1)

        def start(sem, src, owner, r0, n, to):
            cp = remote(
                src, rows_of(owner, r0, n), gs.at[sem], gr.at[sem], {"dp": to}
            )
            cp.start()
            pending.append(cp)

        def relay(sem, owner, r0, n, to):
            start(sem, rows_of(owner, r0, n), owner, r0, n, to)

        def landed(sem, owner, r0, n):
            pltpu.make_async_copy(
                rows_of(owner, r0, n), rows_of(owner, r0, n), gr.at[sem]
            ).wait()

        def blk(r0, n):
            return block.at[pl.ds(r0, n), :]

        start(0, blk(third, RB - third), a, third, RB - third, ACROSS)
        start(1, blk(0, third), a, 0, third, ACROSS)
        start(2, blk(0, half), a, 0, half, UP)
        start(3, blk(half, RB - half), a, half, RB - half, DOWN)
        start(4, blk(half, RB - half), a, half, RB - half, UP)
        start(5, blk(0, half), a, 0, half, DOWN)
        prepare()
        landed(0, ACROSS, third, RB - third)
        relay(6, ACROSS, third, RB - third, UP)
        relay(7, ACROSS, third, RB - third, DOWN)
        landed(2, DOWN, 0, half)
        relay(8, DOWN, 0, half, UP)
        landed(3, UP, half, RB - half)
        relay(9, UP, half, RB - half, DOWN)
        landed(4, DOWN, half, RB - half)
        landed(5, UP, 0, half)
        relay(10, DOWN, 0, third, ACROSS)
        relay(11, UP, 0, third, ACROSS)
        landed(1, ACROSS, 0, third)
        landed(6, at(-1, 1), third, RB - third)
        landed(7, at(1, 1), third, RB - third)
        landed(10, at(-1, 1), 0, third)
        relay(12, at(-1, 1), 0, half, UP)
        landed(11, at(1, 1), 0, third)
        relay(13, at(1, 1), half, RB - half, DOWN)
        landed(8, at(2, 0), 0, half)
        landed(9, at(2, 0), half, RB - half)
        landed(12, at(2, 1), 0, half)
        landed(13, at(2, 1), half, RB - half)
    else:
        for k in range(1, D):
            to = lax.rem(a + k, D)
            cp = remote(block, rows_of(a, 0, RB), gs.at[k], gr.at[k], {"dp": to})
            cp.start()
            pending.append(cp)
        prepare()
        for k in range(1, D):
            of = lax.rem(a - k + D, D)
            pltpu.make_async_copy(rows_of(of, 0, RB), rows_of(of, 0, RB), gr.at[k]).wait()
    own_copy.wait()
    block_copy = pltpu.make_async_copy(block, block_out, out_sem.at[0])
    block_copy.start()

    early = s < (S + 1) // 2

    def flip():
        for part_index in range(2):

            @pl.loop(0, lanes * lanes)
            def _(t):
                i = pl.multiple_of(t // lanes * 128, 128)
                j = pl.multiple_of(lax.rem(t, lanes) * 128, 128)
                flipped[part_index, pl.ds(j, 128), pl.ds(i, 128)] = jnp.transpose(
                    weights[pl.ds(pl.multiple_of(part_index * H + i, 128), 128), pl.ds(j, 128)]
                )

    @pl.when(jnp.logical_not(early))
    def _():
        flip()

    gain_own = gain[c]
    gain_sib = gain[1 - c]

    def w_rows(half_index, chunk):
        at, n = chunk
        return pl.ds(pl.multiple_of(half_index * H + at, 128), n)

    @pl.loop(0, MB)
    def _(b):
        total = jnp.zeros((R, H), F32)
        square = jnp.zeros((R, 1), F32)
        own, other = [], []

        @pl.when(s == 0)
        def _():
            pltpu.make_async_copy(
                tokens.at[b, :, pl.ds(pl.multiple_of(c * H, 128), H)],
                acts.at[b, c],
                local_sem.at[b],
            ).wait()

        for q, (at, n) in enumerate(chunks):
            here = acts.at[b, c, :, pl.ds(at, n)]

            @pl.when(s > 0)
            def _():
                pltpu.make_async_copy(here, here, fr.at[b, q]).wait()

            remote(here, here, rs.at[b, q], rr.at[b, q], sib).start()
            x = acts[b, c, :, at : at + n].astype(F32)
            own.append(x)
            square = square + jnp.sum(x * x, axis=1, keepdims=True)
            total = total + jnp.dot(
                (x * gain_own[:, at : at + n]).astype(BF16),
                weights[w_rows(c, (at, n)), :],
                preferred_element_type=F32,
            )
        for q, (at, n) in enumerate(chunks):
            there = acts.at[b, 1 - c, :, pl.ds(at, n)]
            pltpu.make_async_copy(there, there, rr.at[b, q]).wait()
            x = acts[b, 1 - c, :, at : at + n].astype(F32)
            other.append(x)
            square = square + jnp.sum(x * x, axis=1, keepdims=True)
            x_gain = (x * gain_sib[:, at : at + n]).astype(BF16)
            if q == 0:
                total = total + jnp.dot(
                    x_gain, weights[w_rows(1 - c, (at, n)), :], preferred_element_type=F32
                )
        scale = lax.rsqrt(square * (1.0 / E) + eps_norm)
        for t, (to_at, to_n) in enumerate(chunks):
            pre = (
                total[:, to_at : to_at + to_n]
                + jnp.dot(
                    x_gain,
                    weights[w_rows(1 - c, chunks[1]), to_at : to_at + to_n],
                    preferred_element_type=F32,
                )
            ) * scale
            outs[b, :, to_at : to_at + to_n] = (own[t] + jax.nn.silu(pre)).astype(BF16)

            @pl.when(s < S - 1)
            def _():
                remote(
                    outs.at[b, :, pl.ds(to_at, to_n)],
                    acts.at[b, c, :, pl.ds(to_at, to_n)],
                    fs.at[b, t],
                    fr.at[b, t],
                    {"section": lax.rem(s + 1, S)},
                ).start()

            preacts[b, :, to_at : to_at + to_n] = pre
        scales[b] = jnp.broadcast_to(scale, (R, 128))
        for q, (at, n) in enumerate(chunks):
            cols = slice(at, at + n)
            normed[c, b, :, cols] = (own[q] * scale * gain_own[:, cols]).astype(BF16)
            normed[1 - c, b, :, cols] = (other[q] * scale * gain_sib[:, cols]).astype(BF16)
        for k in range(-(-S // MB)):
            to = b * -(-S // MB) + k

            @pl.when(to < S)
            def _():
                send_piece(m_send, m_recv, ms, mr, to)
                send_piece(v_send, v_recv, vs, vr, to)

    per_half = H // RB

    def window(owner):
        offset = lax.rem(owner, per_half) * RB
        return owner // per_half, pl.multiple_of(offset // 128 * 128, 128)

    def send_features():
        @pl.loop(1, D)
        def _(k):
            to = lax.rem(a + k, D)
            half_index, at = window(to)
            remote(
                normed.at[half_index, :, :, pl.ds(at, width)],
                raw_feats.at[:, a],
                ts.at[to],
                tr.at[a],
                {"dp": to},
            ).start()

        half_index, at = window(a)
        raw_feats[:, a] = normed[half_index, :, :, pl.ds(at, width)]

    send_features()

    def gather_state():
        arrived(m_send, m_recv, ms, mr)
        assemble(m_recv, first)
        pltpu.make_async_copy(first, m_out, out_sem.at[1]).start()
        arrived(v_send, v_recv, vs, vr)
        assemble(v_recv, second)
        pltpu.make_async_copy(second, v_out, out_sem.at[2]).start()

        @pl.loop(1, D)
        def _(k):
            of = lax.rem(a + k, D)
            pltpu.make_async_copy(raw_feats.at[:, of], raw_feats.at[:, of], tr.at[of]).wait()

        @pl.loop(0, MB)
        def _(b):
            for j in range(width // 128):
                feats[b, 128 * j : 128 * (j + 1), :] = jnp.transpose(
                    raw_feats[b, :, :, 128 * j : 128 * (j + 1)].reshape(D * R, 128)
                )

    @pl.when(early)
    def _():
        flip()
        gather_state()

    def dpre_rows(owner, b):
        return dpres.at[pl.ds(pl.multiple_of((b * D + owner) * R, R), R), :]

    my_rem = pl.multiple_of(lax.rem(lax.rem(a, per_half) * RB, 128), 16)

    def weight_grad(pair):
        @pl.loop(1, D)
        def _(k):
            of = lax.rem(a + k, D)
            for b in (2 * pair, 2 * pair + 1):
                pltpu.make_async_copy(dpre_rows(of, b), dpre_rows(of, b), dr.at[b, of]).wait()

        lhs = jnp.concatenate(
            [feats[2 * pair + i, pl.ds(my_rem, RB), :] for i in range(2)], axis=1
        )
        rows = pl.ds(pl.multiple_of(pair * 2 * D * R, 2 * D * R), 2 * D * R)

        def accumulate(cols):
            value = jnp.dot(lhs, dpres[rows, cols], preferred_element_type=F32)

            @pl.when(pair == 0)
            def _():
                grad_out[:, cols] = value

            @pl.when(pair > 0)
            def _():
                grad_out[:, cols] += value

        @pl.loop(0, H // 256)
        def _(j):
            accumulate(pl.ds(pl.multiple_of(j * 256, 128), 256))

        if H % 256:
            accumulate(pl.ds(H - H % 256, H % 256))

    @pl.loop(0, MB)
    def _(b):
        @pl.when(s == S - 1)
        def _():
            pltpu.make_async_copy(
                cotangent.at[b, :, pl.ds(pl.multiple_of(c * H, 128), H)],
                grads_in.at[b],
                local_sem.at[MB + b],
            ).wait()

        def take(q, at, n):
            here = grads_in.at[b, :, pl.ds(at, n)]

            @pl.when(s < S - 1)
            def _():
                pltpu.make_async_copy(here, here, br.at[b, q]).wait()

            upstream = grads_in[b, :, at : at + n].astype(F32)
            pre = preacts[b, :, at : at + n]
            sig = jax.nn.sigmoid(pre)
            dpre = (upstream * (sig * (1.0 + pre * (1.0 - sig)))).astype(BF16)
            dpres[pl.ds(pl.multiple_of((b * D + a) * R, R), R), at : at + n] = dpre
            return upstream, pre, dpre

        @pl.when(s == 0)
        def _():
            for q, (at, n) in enumerate(chunks):
                take(q, at, n)

        @pl.when(s > 0)
        def _():
            ups = []
            stat = jnp.zeros((R, 1), F32)
            for q, (at, n) in enumerate(chunks):
                upstream, pre, dpre = take(q, at, n)
                ups.append(upstream)
                stat = stat + jnp.sum(dpre.astype(F32) * pre, axis=1, keepdims=True)
                if q == 0:
                    away = jnp.dot(
                        dpre, flipped[1 - c, at : at + n, :], preferred_element_type=F32
                    )
                    home = jnp.dot(dpre, flipped[c, at : at + n, :], preferred_element_type=F32)
            stat_send[b] = jnp.broadcast_to(stat, (R, 128))
            remote(stat_send.at[b], stat_recv.at[b], ss.at[b], sr.at[b], sib).start()
            rows = slice(chunks[1][0], H)
            for t, (at, n) in enumerate(chunks):
                part_send[b, :, at : at + n] = (
                    away[:, at : at + n]
                    + jnp.dot(
                        dpre, flipped[1 - c, rows, at : at + n], preferred_element_type=F32
                    )
                ).astype(BF16)
                remote(
                    part_send.at[b, :, pl.ds(at, n)],
                    part_recv.at[b, :, pl.ds(at, n)],
                    ps.at[b, t],
                    pr.at[b, t],
                    sib,
                ).start()
            home = home + jnp.dot(dpre, flipped[c, rows, :], preferred_element_type=F32)
            pltpu.make_async_copy(stat_send.at[b], stat_recv.at[b], sr.at[b]).wait()
            scale = scales[b][:, :1]
            shrink = scale * scale * ((stat + stat_recv[b][:, :1]) * (1.0 / E))
            for t, (at, n) in enumerate(chunks):
                cols = slice(at, at + n)
                there = part_recv.at[b, :, pl.ds(at, n)]
                pltpu.make_async_copy(there, there, pr.at[b, t]).wait()
                dnormed = home[:, cols] + part_recv[b, :, cols].astype(F32)
                back = (
                    ups[t]
                    + scale * (gain_own[:, cols] * dnormed)
                    - acts[b, c, :, cols].astype(F32) * shrink
                )
                grads_out[b, :, cols] = back.astype(BF16)
                remote(
                    grads_out.at[b, :, pl.ds(at, n)],
                    grads_in.at[b, :, pl.ds(at, n)],
                    bs.at[b, t],
                    br.at[b, t],
                    {"section": lax.rem(s + S - 1, S)},
                ).start()

        @pl.loop(1, D)
        def _(k):
            to = lax.rem(a + k, D)
            remote(
                dpre_rows(a, b), dpre_rows(a, b), ds.at[b, to], dr.at[b, a], {"dp": to}
            ).start()

        @pl.when((s == 0) & (b >= 3) & (lax.rem(b, 2) == 1))
        def _():
            weight_grad((b - 3) // 2)

    @pl.when(jnp.logical_not(early))
    def _():
        gather_state()

    @pl.loop(jnp.where(s == 0, MB // 2 - 1, 0), MB // 2)
    def _(pair):
        weight_grad(pair)

    block_copy.wait()
    pltpu.make_async_copy(first, m_out, out_sem.at[1]).wait()
    pltpu.make_async_copy(second, v_out, out_sem.at[2]).wait()
    drained(w_send, w_recv, ws, wr)
    drained(m_send, m_recv, ms, mr)
    drained(v_send, v_recv, vs, vr)
    for cp in pending:
        cp.wait_send()

    @pl.loop(0, MB)
    def _(b):
        for q, (at, n) in enumerate(chunks):
            here = acts.at[b, c, :, pl.ds(at, n)]
            remote(here, here, rs.at[b, q], rr.at[b, q], sib).wait_send()

            @pl.when(s < S - 1)
            def _():
                out = outs.at[b, :, pl.ds(at, n)]
                remote(out, here, fs.at[b, q], fr.at[b, q], sib).wait_send()

            @pl.when(s > 0)
            def _():
                part = part_send.at[b, :, pl.ds(at, n)]
                remote(
                    part, part_recv.at[b, :, pl.ds(at, n)], ps.at[b, q], pr.at[b, q], sib
                ).wait_send()
                back = grads_out.at[b, :, pl.ds(at, n)]
                remote(
                    back, grads_in.at[b, :, pl.ds(at, n)], bs.at[b, q], br.at[b, q], sib
                ).wait_send()

        @pl.when(s > 0)
        def _():
            remote(stat_send.at[b], stat_recv.at[b], ss.at[b], sr.at[b], sib).wait_send()

        @pl.loop(1, D)
        def _(k):
            to = lax.rem(a + k, D)
            remote(
                dpre_rows(a, b), dpre_rows(a, b), ds.at[b, to], dr.at[b, a], {"dp": to}
            ).wait_send()

    @pl.loop(1, D)
    def _(k):
        to = lax.rem(a + k, D)
        half_index, at = window(to)
        remote(
            normed.at[half_index, :, :, pl.ds(at, width)],
            raw_feats.at[:, a],
            ts.at[to],
            tr.at[a],
            {"dp": to},
        ).wait_send()


def local(old_w, old_m, old_v, old_slot_layer, norm_gain, tokens, cotangent):
    S = lax.axis_size("section")
    D = lax.axis_size("dp")
    PR, H = old_w.shape[3], old_w.shape[4]
    MB, R = tokens.shape[0], tokens.shape[1]
    RB = S * PR
    TOK = MB * R
    E = 2 * H
    layer_ids = jnp.arange(S, dtype=jnp.int32)
    matches = (old_slot_layer[None, :] == layer_ids[:, None]).astype(jnp.int32)
    order = jnp.sum(matches * layer_ids[None, :], axis=1)
    vmem = pl.BlockSpec(memory_space=pltpu.VMEM)
    anyspace = pl.BlockSpec(memory_space=pl.ANY)
    dma = pltpu.SemaphoreType.DMA
    padded = -(-PR // 16) * 16
    width = feature_width(RB, H)
    grad, master, moment, square = pl.pallas_call(
        functools.partial(kernel, (S, D, PR, H, MB, R)),
        out_shape=(
            jax.ShapeDtypeStruct((RB, H), F32),
            jax.ShapeDtypeStruct((RB, H), BF16),
            jax.ShapeDtypeStruct((RB, H), BF16),
            jax.ShapeDtypeStruct((RB, H), BF16),
        ),
        in_specs=[pl.BlockSpec(memory_space=pltpu.SMEM), vmem, vmem, vmem, vmem, anyspace, anyspace],
        out_specs=(vmem, anyspace, anyspace, anyspace),
        scratch_shapes=[
            pltpu.VMEM((S, PR, H), BF16),
            pltpu.VMEM((S, padded, H), BF16),
            pltpu.VMEM((S, padded, H), BF16),
            pltpu.VMEM((S, PR, H), BF16),
            pltpu.VMEM((S, padded, H), BF16),
            pltpu.VMEM((S, padded, H), BF16),
            pltpu.VMEM((S * padded, PR * S), BF16),
            pltpu.VMEM((RB, 128), F32),
            pltpu.VMEM((RB, H), BF16),
            pltpu.VMEM((RB, H), BF16),
            pltpu.VMEM((RB, H), BF16),
            pltpu.VMEM((E, H), BF16),
            pltpu.VMEM((2, H, H), BF16),
            pltpu.VMEM((MB, 2, R, H), BF16),
            pltpu.VMEM((MB, R, H), BF16),
            pltpu.VMEM((MB, R, H), F32),
            pltpu.VMEM((MB, R, 128), F32),
            pltpu.VMEM((2, MB, R, H), BF16),
            pltpu.VMEM((MB, D, R, width), BF16),
            pltpu.VMEM((MB, width, D * R), BF16),
            pltpu.VMEM((MB, R, H), BF16),
            pltpu.VMEM((MB, R, H), BF16),
            pltpu.VMEM((D * TOK, H), BF16),
            pltpu.VMEM((MB, R, H), BF16),
            pltpu.VMEM((MB, R, H), BF16),
            pltpu.VMEM((MB, R, 128), F32),
            pltpu.VMEM((MB, R, 128), F32),
            dma((S,)),
            dma((S,)),
            dma((S,)),
            dma((S,)),
            dma((S,)),
            dma((S,)),
            dma((14,)),
            dma((14,)),
            dma((MB, 2)),
            dma((MB, 2)),
            dma((MB, 2)),
            dma((MB, 2)),
            dma((MB, 2)),
            dma((MB, 2)),
            dma((MB,)),
            dma((MB,)),
            dma((MB, 2)),
            dma((MB, 2)),
            dma((D,)),
            dma((D,)),
            dma((MB, D)),
            dma((MB, D)),
            dma((2 * MB + 1,)),
            dma((3,)),
        ],
        compiler_params=pltpu.CompilerParams(
            collective_id=0, has_side_effects=True, vmem_limit_bytes=63_000_000
        ),
    )(
        order,
        old_w.reshape(S * PR * H // 128, 128),
        old_m.reshape(S, PR, H).transpose(1, 0, 2),
        old_v.reshape(S, PR, H).transpose(1, 0, 2),
        norm_gain.reshape(2, 1, H),
        tokens,
        cotangent,
    )
    moment_next = beta_one * moment.astype(F32) + (1.0 - beta_one) * grad
    second_next = beta_two * square.astype(F32) + (1.0 - beta_two) * grad * grad
    fix_one = 1.0 - beta_one**step_count
    fix_two = 1.0 - beta_two**step_count
    direction = moment_next / fix_one / (jnp.sqrt(second_next / fix_two) + adam_eps)
    kept = master.astype(F32)
    updated = kept - learn_rate * (direction + decay_rate * kept)
    return updated[None], moment_next.astype(BF16)[None], second_next.astype(BF16)[None]


def solution(mesh):
    placed = (
        P(None, "dp", "section", None, "mp"),
        P(None, "dp", "section", None, "mp"),
        P(None, "dp", "section", None, "mp"),
        P(),
        P("section", None),
        P(None, "dp", None),
        P(None, "dp", None),
    )
    return jax.shard_map(
        local,
        mesh=mesh,
        in_specs=placed,
        out_specs=(P("section", "dp", "mp"), P("section", "dp", "mp"), P("section", "dp", "mp")),
        check_vma=False,
    )
```

```python
import functools

import jax
import jax.numpy as jnp
from jax import lax
from jax.experimental import pallas as pl
from jax.experimental.pallas import tpu as pltpu
from jax.sharding import PartitionSpec as P

eps_norm = 1e-05
beta_one = 0.9
beta_two = 0.95
learn_rate = 0.001
decay_rate = 0.1
adam_eps = 1e-08
step_count = 1000.0

MESH = pl.DeviceIdType.MESH
F32 = jnp.float32
BF16 = jnp.bfloat16
XS = 4


def remote(src, dst, send_sem, recv_sem, device):
    return pltpu.make_async_remote_copy(
        src_ref=src,
        dst_ref=dst,
        send_sem=send_sem,
        recv_sem=recv_sem,
        device_id=device,
        device_id_type=MESH,
    )


def relay_plan(rows):
    two_thirds = max(16, (rows * 2 // 3 + 15) // 16 * 16)
    half = (rows // 2 + 15) // 16 * 16
    return two_thirds, half


def feature_width(rows, half):
    return max(
        -(-(rows * k % 128 + rows) // 128) * 128 for k in range(half // rows)
    )


def kernel(
    sizes,
    order,
    old_w,
    old_m,
    old_v,
    gain,
    tokens,
    cotangent,
    grad_out,
    block_out,
    m_out,
    v_out,
    w_send,
    m_send,
    v_send,
    w_recv,
    m_recv,
    v_recv,
    pick,
    wide,
    block,
    first,
    second,
    weights,
    flipped,
    acts,
    outs,
    preacts,
    scales,
    normed,
    raw_feats,
    feats,
    grads_in,
    grads_out,
    dpres,
    part_send,
    part_recv,
    stat_send,
    stat_recv,
    ws,
    wr,
    ms,
    mr,
    vs,
    vr,
    gs,
    gr,
    fs,
    fr,
    rs,
    rr,
    ps,
    pr,
    ss,
    sr,
    bs,
    br,
    ts,
    tr,
    ds,
    dr,
    local_sem,
    out_sem,
):
    S, D, pr_rows, H, MB, R = sizes
    RB = S * pr_rows
    TOK = MB * R
    E = 2 * H
    s = lax.axis_index("section")
    a = lax.axis_index("dp")
    c = lax.axis_index("mp")
    sib = {"mp": 1 - c}
    lanes = H // 128
    cut = (lanes + 1) // 2 * 128
    chunks = ((0, cut), (cut, H - cut))
    width = feature_width(RB, H)
    rounds = 2 if S % 2 == 0 and RB // 2 % 16 == 0 else 1
    G, GR = S // rounds, RB // rounds
    group = s // G
    spot = lax.rem(s, G)
    groups = [group, 1 - group][:rounds]
    near = sorted(range(1, G), key=lambda k: min(k, G - k))

    barrier = pltpu.get_barrier_semaphore()

    @pl.loop(1, S)
    def _(k):
        pl.semaphore_signal(
            barrier, inc=1, device_id={"section": lax.rem(s + k, S)}, device_id_type=MESH
        )

    @pl.loop(1, D)
    def _(k):
        pl.semaphore_signal(
            barrier, inc=1, device_id={"dp": lax.rem(a + k, D)}, device_id_type=MESH
        )

    pl.semaphore_signal(barrier, inc=1, device_id=sib, device_id_type=MESH)

    @pl.when(s == 0)
    def _():
        @pl.loop(0, MB)
        def _(b):
            pltpu.make_async_copy(
                tokens.at[b, :, pl.ds(pl.multiple_of(c * H, 128), H)],
                acts.at[b, c],
                local_sem.at[b],
            ).start()

    @pl.when(s == S - 1)
    def _():
        @pl.loop(0, MB)
        def _(b):
            pltpu.make_async_copy(
                cotangent.at[b, :, pl.ds(pl.multiple_of(c * H, 128), H)],
                grads_in.at[b],
                local_sem.at[MB + b],
            ).start()

    @pl.loop(0, S)
    def _(k):
        base = order[k] * (pr_rows * lanes)
        for j in range(lanes):
            w_send[k, :, 128 * j : 128 * (j + 1)] = old_w[
                pl.ds(base + j, pr_rows, stride=lanes), :
            ].astype(BF16)

    pl.semaphore_wait(barrier, S + D - 1)

    def send_piece(send, recv, send_sems, recv_sems, to):
        remote(
            send.at[to], recv.at[s], send_sems.at[to], recv_sems.at[s], {"section": to}
        ).start()

    def peers(which, offsets):
        return [groups[which] * G + lax.rem(spot + k, G) for k in offsets]

    def arrived(send, recv, send_sems, recv_sems, which):
        for of in peers(which, near if which == 0 else range(G)):
            remote(
                send.at[of], recv.at[of], send_sems.at[of], recv_sems.at[of], {"section": of}
            ).wait_recv()

    def drained(send, recv, send_sems, recv_sems):
        @pl.loop(1, S)
        def _(k):
            of = lax.rem(s + k, S)
            remote(
                send.at[of], recv.at[of], send_sems.at[of], recv_sems.at[of], {"section": of}
            ).wait_send()

    def assemble(recv, dst, which):
        base = groups[which] * G
        rows = pl.ds(pl.multiple_of(groups[which] * GR, 16), GR)

        @pl.loop(0, lanes)
        def _(j):
            cols = pl.ds(pl.multiple_of(j * 128, 128), 128)
            for i in range(G):
                wide[pr_rows * i : pr_rows * (i + 1), :] = recv[
                    base + i, 0:pr_rows, cols
                ].astype(F32)
            dst[rows, cols] = wide[...].astype(BF16)

    for which in range(rounds):
        for to in peers(which, near if which == 0 else [0] + near):
            send_piece(w_send, w_recv, ws, wr, to)

    w_recv[s] = w_send[s]

    def rows_of(owner, r0, n):
        return weights.at[pl.ds(pl.multiple_of(owner * RB + r0, 16), n), :]

    def prepare():
        padded = m_send.shape[1]

        @pl.loop(0, S)
        def _(k):
            shape = (padded, pr_rows * S)
            row = lax.broadcasted_iota(jnp.int32, shape, 0)
            col = lax.broadcasted_iota(jnp.int32, shape, 1)
            hit = col == row * S + order[k]
            pick[pl.ds(pl.multiple_of(k * padded, 16), padded), :] = jnp.where(
                hit & (row < pr_rows), 1.0, 0.0
            ).astype(BF16)

        def select(old, send):
            @pl.loop(0, lanes)
            def _(j):
                cols = pl.ds(pl.multiple_of(j * 128, 128), 128)
                flat = old[:, :, cols].reshape(pr_rows * S, 128)
                send[:, :, cols] = (
                    jnp.dot(pick[...], flat, preferred_element_type=F32)
                    .astype(BF16)
                    .reshape(S, padded, 128)
                )

        select(old_m, m_send)
        select(old_v, v_send)
        m_recv[s] = m_send[s]
        v_recv[s] = v_send[s]

    pending = []

    def begin(which):
        arrived(w_send, w_recv, ws, wr, which)
        assemble(w_recv, block, which)
        at = pl.multiple_of(groups[which] * GR, 16)
        own = pltpu.make_async_copy(
            block.at[pl.ds(at, GR), :], rows_of(a, at, GR), local_sem.at[2 * MB + which]
        )
        own.start()
        return own

    def relays(which):
        x = lax.rem(a, XS)
        h = a // XS
        base = pl.multiple_of(groups[which] * GR, 16)

        def at(dx, dh):
            hh = (1 - h) if dh else h
            return hh * XS + lax.rem(x + dx + XS, XS)

        third, half = relay_plan(GR)
        up, down, across = at(1, 0), at(-1, 0), at(0, 1)

        def start(sem, src, owner, r0, n, to):
            sem = sem + 14 * which
            cp = remote(
                src, rows_of(owner, base + r0, n), gs.at[sem], gr.at[sem], {"dp": to}
            )
            cp.start()
            pending.append(cp)

        def relay(sem, owner, r0, n, to):
            start(sem, rows_of(owner, base + r0, n), owner, r0, n, to)

        def landed(sem, owner, r0, n):
            there = rows_of(owner, base + r0, n)
            pltpu.make_async_copy(there, there, gr.at[sem + 14 * which]).wait()

        def blk(r0, n):
            return block.at[pl.ds(pl.multiple_of(base + r0, 16), n), :]

        begun = begin(which)
        start(0, blk(third, GR - third), a, third, GR - third, across)
        start(1, blk(0, third), a, 0, third, across)
        start(2, blk(0, half), a, 0, half, up)
        start(3, blk(half, GR - half), a, half, GR - half, down)
        start(4, blk(half, GR - half), a, half, GR - half, up)
        start(5, blk(0, half), a, 0, half, down)
        yield
        landed(0, across, third, GR - third)
        relay(6, across, third, GR - third, up)
        relay(7, across, third, GR - third, down)
        landed(2, down, 0, half)
        relay(8, down, 0, half, up)
        landed(3, up, half, GR - half)
        relay(9, up, half, GR - half, down)
        yield
        landed(4, down, half, GR - half)
        relay(10, down, 0, third, across)
        landed(5, up, 0, half)
        relay(11, up, 0, third, across)
        yield
        landed(1, across, 0, third)
        landed(6, at(-1, 1), third, GR - third)
        landed(10, at(-1, 1), 0, third)
        relay(12, at(-1, 1), 0, half, up)
        landed(7, at(1, 1), third, GR - third)
        landed(11, at(1, 1), 0, third)
        relay(13, at(1, 1), half, GR - half, down)
        yield
        landed(8, at(2, 0), 0, half)
        landed(9, at(2, 0), half, GR - half)
        landed(12, at(2, 1), 0, half)
        landed(13, at(2, 1), half, GR - half)
        begun.wait()
        yield

    def direct(which):
        base = pl.multiple_of(groups[which] * GR, 16)
        begun = begin(which)
        for k in range(1, D):
            to = lax.rem(a + k, D)
            sem = k + 14 * which
            cp = remote(
                block.at[pl.ds(base, GR), :],
                rows_of(a, base, GR),
                gs.at[sem],
                gr.at[sem],
                {"dp": to},
            )
            cp.start()
            pending.append(cp)
        yield
        for k in range(1, D):
            there = rows_of(lax.rem(a - k + D, D), base, GR)
            pltpu.make_async_copy(there, there, gr.at[k + 14 * which]).wait()
        begun.wait()
        for _ in range(4):
            yield

    def moments(which, offsets):
        for to in peers(which, offsets):
            send_piece(m_send, m_recv, ms, mr, to)
            send_piece(v_send, v_recv, vs, vr, to)

    routes = [(relays if D == 2 * XS else direct)(which) for which in range(rounds)]
    next(routes[0])
    prepare()
    moments(0, near)
    if rounds == 1:
        for _ in routes[0]:
            pass
    else:
        for which in (0, 1, 0, 1, 0, 1, 0, 1, 1):
            next(routes[which])

    block_copy = pltpu.make_async_copy(block, block_out, out_sem.at[0])
    block_copy.start()

    early = s < (S + 1) // 2

    def flip():
        for part_index in range(2):

            @pl.loop(0, lanes * lanes)
            def _(t):
                i = pl.multiple_of(t // lanes * 128, 128)
                j = pl.multiple_of(lax.rem(t, lanes) * 128, 128)
                flipped[part_index, pl.ds(j, 128), pl.ds(i, 128)] = jnp.transpose(
                    weights[pl.ds(pl.multiple_of(part_index * H + i, 128), 128), pl.ds(j, 128)]
                )

    behind = [0] + [k for k in near if 2 * k > G]
    ahead = [k for k in near if 2 * k <= G]
    if rounds == 2:
        moments(1, behind)

    @pl.when(jnp.logical_not(early))
    def _():
        flip()
        if rounds == 2:
            moments(1, ahead)

    gain_own = gain[c]
    gain_sib = gain[1 - c]

    def w_rows(half_index, chunk):
        at, n = chunk
        return pl.ds(pl.multiple_of(half_index * H + at, 128), n)

    @pl.loop(0, MB)
    def _(b):
        total = jnp.zeros((R, H), F32)
        square = jnp.zeros((R, 1), F32)
        own, other = [], []

        @pl.when(s == 0)
        def _():
            pltpu.make_async_copy(
                tokens.at[b, :, pl.ds(pl.multiple_of(c * H, 128), H)],
                acts.at[b, c],
                local_sem.at[b],
            ).wait()

        for q, (at, n) in enumerate(chunks):
            here = acts.at[b, c, :, pl.ds(at, n)]

            @pl.when(s > 0)
            def _():
                pltpu.make_async_copy(here, here, fr.at[b, q]).wait()

            remote(here, here, rs.at[b, q], rr.at[b, q], sib).start()
            x = acts[b, c, :, at : at + n].astype(F32)
            own.append(x)
            square = square + jnp.sum(x * x, axis=1, keepdims=True)
            total = total + jnp.dot(
                (x * gain_own[:, at : at + n]).astype(BF16),
                weights[w_rows(c, (at, n)), :],
                preferred_element_type=F32,
            )
        for q, (at, n) in enumerate(chunks):
            there = acts.at[b, 1 - c, :, pl.ds(at, n)]
            pltpu.make_async_copy(there, there, rr.at[b, q]).wait()
            x = acts[b, 1 - c, :, at : at + n].astype(F32)
            other.append(x)
            square = square + jnp.sum(x * x, axis=1, keepdims=True)
            x_gain = (x * gain_sib[:, at : at + n]).astype(BF16)
            if q == 0:
                total = total + jnp.dot(
                    x_gain, weights[w_rows(1 - c, (at, n)), :], preferred_element_type=F32
                )
        scale = lax.rsqrt(square * (1.0 / E) + eps_norm)
        for t, (to_at, to_n) in enumerate(chunks):
            pre = (
                total[:, to_at : to_at + to_n]
                + jnp.dot(
                    x_gain,
                    weights[w_rows(1 - c, chunks[1]), to_at : to_at + to_n],
                    preferred_element_type=F32,
                )
            ) * scale
            outs[b, :, to_at : to_at + to_n] = (own[t] + jax.nn.silu(pre)).astype(BF16)

            @pl.when(s < S - 1)
            def _():
                remote(
                    outs.at[b, :, pl.ds(to_at, to_n)],
                    acts.at[b, c, :, pl.ds(to_at, to_n)],
                    fs.at[b, t],
                    fr.at[b, t],
                    {"section": lax.rem(s + 1, S)},
                ).start()

            preacts[b, :, to_at : to_at + to_n] = pre
        scales[b] = jnp.broadcast_to(scale, (R, 128))
        for q, (at, n) in enumerate(chunks):
            cols = slice(at, at + n)
            normed[c, b, :, cols] = (own[q] * scale * gain_own[:, cols]).astype(BF16)
            normed[1 - c, b, :, cols] = (other[q] * scale * gain_sib[:, cols]).astype(BF16)

    per_half = H // RB

    def window(owner):
        offset = lax.rem(owner, per_half) * RB
        return owner // per_half, pl.multiple_of(offset // 128 * 128, 128)

    def send_features():
        @pl.loop(1, D)
        def _(k):
            to = lax.rem(a + k, D)
            half_index, at = window(to)
            remote(
                normed.at[half_index, :, :, pl.ds(at, width)],
                raw_feats.at[:, a],
                ts.at[to],
                tr.at[a],
                {"dp": to},
            ).start()

        half_index, at = window(a)
        raw_feats[:, a] = normed[half_index, :, :, pl.ds(at, width)]

    send_features()

    def gather_state():
        for which in range(rounds):
            arrived(m_send, m_recv, ms, mr, which)
            assemble(m_recv, first, which)
        pltpu.make_async_copy(first, m_out, out_sem.at[1]).start()
        for which in range(rounds):
            arrived(v_send, v_recv, vs, vr, which)
            assemble(v_recv, second, which)
        pltpu.make_async_copy(second, v_out, out_sem.at[2]).start()

        @pl.loop(1, D)
        def _(k):
            of = lax.rem(a + k, D)
            pltpu.make_async_copy(raw_feats.at[:, of], raw_feats.at[:, of], tr.at[of]).wait()

        @pl.loop(0, MB)
        def _(b):
            for j in range(width // 128):
                feats[b, 128 * j : 128 * (j + 1), :] = jnp.transpose(
                    raw_feats[b, :, :, 128 * j : 128 * (j + 1)].reshape(D * R, 128)
                )

    @pl.when(early)
    def _():
        flip()
        if rounds == 2:
            moments(1, ahead)

    soon = s < max(1, S // 4)

    @pl.when(soon)
    def _():
        gather_state()

    def dpre_rows(owner, b):
        return dpres.at[pl.ds(pl.multiple_of((b * D + owner) * R, R), R), :]

    my_rem = pl.multiple_of(lax.rem(lax.rem(a, per_half) * RB, 128), 16)

    def weight_grad(pair):
        @pl.loop(1, D)
        def _(k):
            of = lax.rem(a + k, D)
            for b in (2 * pair, 2 * pair + 1):
                pltpu.make_async_copy(dpre_rows(of, b), dpre_rows(of, b), dr.at[b, of]).wait()

        lhs = jnp.concatenate(
            [feats[2 * pair + i, pl.ds(my_rem, RB), :] for i in range(2)], axis=1
        )
        rows = pl.ds(pl.multiple_of(pair * 2 * D * R, 2 * D * R), 2 * D * R)

        def accumulate(cols):
            value = jnp.dot(lhs, dpres[rows, cols], preferred_element_type=F32)

            @pl.when(pair == 0)
            def _():
                grad_out[:, cols] = value

            @pl.when(pair > 0)
            def _():
                grad_out[:, cols] += value

        @pl.loop(0, H // 256)
        def _(j):
            accumulate(pl.ds(pl.multiple_of(j * 256, 128), 256))

        if H % 256:
            accumulate(pl.ds(H - H % 256, H % 256))

    @pl.loop(0, MB)
    def _(b):
        @pl.when(s == S - 1)
        def _():
            pltpu.make_async_copy(
                cotangent.at[b, :, pl.ds(pl.multiple_of(c * H, 128), H)],
                grads_in.at[b],
                local_sem.at[MB + b],
            ).wait()

        def take(q, at, n):
            here = grads_in.at[b, :, pl.ds(at, n)]

            @pl.when(s < S - 1)
            def _():
                pltpu.make_async_copy(here, here, br.at[b, q]).wait()

            upstream = grads_in[b, :, at : at + n].astype(F32)
            pre = preacts[b, :, at : at + n]
            sig = jax.nn.sigmoid(pre)
            dpre = (upstream * (sig * (1.0 + pre * (1.0 - sig)))).astype(BF16)
            dpres[pl.ds(pl.multiple_of((b * D + a) * R, R), R), at : at + n] = dpre
            return upstream, pre, dpre

        @pl.when(s == 0)
        def _():
            for q, (at, n) in enumerate(chunks):
                take(q, at, n)

        @pl.when(s > 0)
        def _():
            ups = []
            stat = jnp.zeros((R, 1), F32)
            for q, (at, n) in enumerate(chunks):
                upstream, pre, dpre = take(q, at, n)
                ups.append(upstream)
                stat = stat + jnp.sum(dpre.astype(F32) * pre, axis=1, keepdims=True)
                if q == 0:
                    away = jnp.dot(
                        dpre, flipped[1 - c, at : at + n, :], preferred_element_type=F32
                    )
                    home = jnp.dot(dpre, flipped[c, at : at + n, :], preferred_element_type=F32)
            stat_send[b] = jnp.broadcast_to(stat, (R, 128))
            remote(stat_send.at[b], stat_recv.at[b], ss.at[b], sr.at[b], sib).start()
            rows = slice(chunks[1][0], H)
            for t, (at, n) in enumerate(chunks):
                part_send[b, :, at : at + n] = (
                    away[:, at : at + n]
                    + jnp.dot(
                        dpre, flipped[1 - c, rows, at : at + n], preferred_element_type=F32
                    )
                ).astype(BF16)
                remote(
                    part_send.at[b, :, pl.ds(at, n)],
                    part_recv.at[b, :, pl.ds(at, n)],
                    ps.at[b, t],
                    pr.at[b, t],
                    sib,
                ).start()
            home = home + jnp.dot(dpre, flipped[c, rows, :], preferred_element_type=F32)
            pltpu.make_async_copy(stat_send.at[b], stat_recv.at[b], sr.at[b]).wait()
            scale = scales[b][:, :1]
            shrink = scale * scale * ((stat + stat_recv[b][:, :1]) * (1.0 / E))
            for t, (at, n) in enumerate(chunks):
                cols = slice(at, at + n)
                there = part_recv.at[b, :, pl.ds(at, n)]
                pltpu.make_async_copy(there, there, pr.at[b, t]).wait()
                dnormed = home[:, cols] + part_recv[b, :, cols].astype(F32)
                back = (
                    ups[t]
                    + scale * (gain_own[:, cols] * dnormed)
                    - acts[b, c, :, cols].astype(F32) * shrink
                )
                grads_out[b, :, cols] = back.astype(BF16)
                remote(
                    grads_out.at[b, :, pl.ds(at, n)],
                    grads_in.at[b, :, pl.ds(at, n)],
                    bs.at[b, t],
                    br.at[b, t],
                    {"section": lax.rem(s + S - 1, S)},
                ).start()

        @pl.loop(1, D)
        def _(k):
            to = lax.rem(a + k, D)
            remote(
                dpre_rows(a, b), dpre_rows(a, b), ds.at[b, to], dr.at[b, a], {"dp": to}
            ).start()

        @pl.when((s == 0) & (b >= 3) & (lax.rem(b, 2) == 1))
        def _():
            weight_grad((b - 3) // 2)

    @pl.when(jnp.logical_not(soon))
    def _():
        gather_state()

    @pl.loop(jnp.where(s == 0, MB // 2 - 1, 0), MB // 2)
    def _(pair):
        weight_grad(pair)

    block_copy.wait()
    pltpu.make_async_copy(first, m_out, out_sem.at[1]).wait()
    pltpu.make_async_copy(second, v_out, out_sem.at[2]).wait()
    drained(w_send, w_recv, ws, wr)
    drained(m_send, m_recv, ms, mr)
    drained(v_send, v_recv, vs, vr)
    for cp in pending:
        cp.wait_send()

    @pl.loop(0, MB)
    def _(b):
        for q, (at, n) in enumerate(chunks):
            here = acts.at[b, c, :, pl.ds(at, n)]
            remote(here, here, rs.at[b, q], rr.at[b, q], sib).wait_send()

            @pl.when(s < S - 1)
            def _():
                out = outs.at[b, :, pl.ds(at, n)]
                remote(out, here, fs.at[b, q], fr.at[b, q], sib).wait_send()

            @pl.when(s > 0)
            def _():
                part = part_send.at[b, :, pl.ds(at, n)]
                remote(
                    part, part_recv.at[b, :, pl.ds(at, n)], ps.at[b, q], pr.at[b, q], sib
                ).wait_send()
                back = grads_out.at[b, :, pl.ds(at, n)]
                remote(
                    back, grads_in.at[b, :, pl.ds(at, n)], bs.at[b, q], br.at[b, q], sib
                ).wait_send()

        @pl.when(s > 0)
        def _():
            remote(stat_send.at[b], stat_recv.at[b], ss.at[b], sr.at[b], sib).wait_send()

        @pl.loop(1, D)
        def _(k):
            to = lax.rem(a + k, D)
            remote(
                dpre_rows(a, b), dpre_rows(a, b), ds.at[b, to], dr.at[b, a], {"dp": to}
            ).wait_send()

    @pl.loop(1, D)
    def _(k):
        to = lax.rem(a + k, D)
        half_index, at = window(to)
        remote(
            normed.at[half_index, :, :, pl.ds(at, width)],
            raw_feats.at[:, a],
            ts.at[to],
            tr.at[a],
            {"dp": to},
        ).wait_send()


def local(old_w, old_m, old_v, old_slot_layer, norm_gain, tokens, cotangent):
    S = lax.axis_size("section")
    D = lax.axis_size("dp")
    PR, H = old_w.shape[3], old_w.shape[4]
    MB, R = tokens.shape[0], tokens.shape[1]
    RB = S * PR
    TOK = MB * R
    E = 2 * H
    layer_ids = jnp.arange(S, dtype=jnp.int32)
    matches = (old_slot_layer[None, :] == layer_ids[:, None]).astype(jnp.int32)
    order = jnp.sum(matches * layer_ids[None, :], axis=1)
    vmem = pl.BlockSpec(memory_space=pltpu.VMEM)
    anyspace = pl.BlockSpec(memory_space=pl.ANY)
    dma = pltpu.SemaphoreType.DMA
    padded = -(-PR // 16) * 16
    group_rows = RB // 2 if S % 2 == 0 and RB // 2 % 16 == 0 else RB
    width = feature_width(RB, H)
    grad, master, moment, square = pl.pallas_call(
        functools.partial(kernel, (S, D, PR, H, MB, R)),
        out_shape=(
            jax.ShapeDtypeStruct((RB, H), F32),
            jax.ShapeDtypeStruct((RB, H), BF16),
            jax.ShapeDtypeStruct((RB, H), BF16),
            jax.ShapeDtypeStruct((RB, H), BF16),
        ),
        in_specs=[pl.BlockSpec(memory_space=pltpu.SMEM), vmem, vmem, vmem, vmem, anyspace, anyspace],
        out_specs=(vmem, anyspace, anyspace, anyspace),
        scratch_shapes=[
            pltpu.VMEM((S, PR, H), BF16),
            pltpu.VMEM((S, padded, H), BF16),
            pltpu.VMEM((S, padded, H), BF16),
            pltpu.VMEM((S, PR, H), BF16),
            pltpu.VMEM((S, padded, H), BF16),
            pltpu.VMEM((S, padded, H), BF16),
            pltpu.VMEM((S * padded, PR * S), BF16),
            pltpu.VMEM((group_rows, 128), F32),
            pltpu.VMEM((RB, H), BF16),
            pltpu.VMEM((RB, H), BF16),
            pltpu.VMEM((RB, H), BF16),
            pltpu.VMEM((E, H), BF16),
            pltpu.VMEM((2, H, H), BF16),
            pltpu.VMEM((MB, 2, R, H), BF16),
            pltpu.VMEM((MB, R, H), BF16),
            pltpu.VMEM((MB, R, H), F32),
            pltpu.VMEM((MB, R, 128), F32),
            pltpu.VMEM((2, MB, R, H), BF16),
            pltpu.VMEM((MB, D, R, width), BF16),
            pltpu.VMEM((MB, width, D * R), BF16),
            pltpu.VMEM((MB, R, H), BF16),
            pltpu.VMEM((MB, R, H), BF16),
            pltpu.VMEM((D * TOK, H), BF16),
            pltpu.VMEM((MB, R, H), BF16),
            pltpu.VMEM((MB, R, H), BF16),
            pltpu.VMEM((MB, R, 128), F32),
            pltpu.VMEM((MB, R, 128), F32),
            dma((S,)),
            dma((S,)),
            dma((S,)),
            dma((S,)),
            dma((S,)),
            dma((S,)),
            dma((28,)),
            dma((28,)),
            dma((MB, 2)),
            dma((MB, 2)),
            dma((MB, 2)),
            dma((MB, 2)),
            dma((MB, 2)),
            dma((MB, 2)),
            dma((MB,)),
            dma((MB,)),
            dma((MB, 2)),
            dma((MB, 2)),
            dma((D,)),
            dma((D,)),
            dma((MB, D)),
            dma((MB, D)),
            dma((2 * MB + 2,)),
            dma((3,)),
        ],
        compiler_params=pltpu.CompilerParams(
            collective_id=0, has_side_effects=True, vmem_limit_bytes=63_000_000
        ),
    )(
        order,
        old_w.reshape(S * PR * H // 128, 128),
        old_m.reshape(S, PR, H).transpose(1, 0, 2),
        old_v.reshape(S, PR, H).transpose(1, 0, 2),
        norm_gain.reshape(2, 1, H),
        tokens,
        cotangent,
    )
    moment_next = beta_one * moment.astype(F32) + (1.0 - beta_one) * grad
    second_next = beta_two * square.astype(F32) + (1.0 - beta_two) * grad * grad
    fix_one = 1.0 - beta_one**step_count
    fix_two = 1.0 - beta_two**step_count
    direction = moment_next / fix_one / (jnp.sqrt(second_next / fix_two) + adam_eps)
    kept = master.astype(F32)
    updated = kept - learn_rate * (direction + decay_rate * kept)
    return updated[None], moment_next.astype(BF16)[None], second_next.astype(BF16)[None]


def solution(mesh):
    placed = (
        P(None, "dp", "section", None, "mp"),
        P(None, "dp", "section", None, "mp"),
        P(None, "dp", "section", None, "mp"),
        P(),
        P("section", None),
        P(None, "dp", None),
        P(None, "dp", None),
    )
    return jax.shard_map(
        local,
        mesh=mesh,
        in_specs=placed,
        out_specs=(P("section", "dp", "mp"), P("section", "dp", "mp"), P("section", "dp", "mp")),
        check_vma=False,
    )
```

```python
import functools

import jax
import jax.numpy as jnp
from jax import lax
from jax.experimental import pallas as pl
from jax.experimental.pallas import tpu as pltpu
from jax.sharding import PartitionSpec as P

eps_norm = 1e-05
beta_one = 0.9
beta_two = 0.95
learn_rate = 0.001
decay_rate = 0.1
adam_eps = 1e-08
step_count = 1000.0

MESH = pl.DeviceIdType.MESH
F32 = jnp.float32
BF16 = jnp.bfloat16
XS = 4


def remote(src, dst, send_sem, recv_sem, device):
    return pltpu.make_async_remote_copy(
        src_ref=src,
        dst_ref=dst,
        send_sem=send_sem,
        recv_sem=recv_sem,
        device_id=device,
        device_id_type=MESH,
    )


def relay_plan(rows):
    two_thirds = max(16, (rows * 2 // 3 + 15) // 16 * 16)
    half = (rows // 2 + 15) // 16 * 16
    return two_thirds, half


def feature_width(rows, half):
    return max(
        -(-(rows * k % 128 + rows) // 128) * 128 for k in range(half // rows)
    )


def kernel(
    sizes,
    order,
    old_w_hbm,
    old_m_hbm,
    old_v_hbm,
    gain,
    tokens,
    cotangent,
    grad_out,
    block_out,
    m_out,
    v_out,
    old_w,
    old_m,
    old_v,
    w_send,
    m_send,
    v_send,
    w_recv,
    m_recv,
    v_recv,
    pick,
    wide,
    block,
    first,
    second,
    weights,
    flipped,
    acts,
    outs,
    preacts,
    scales,
    normed,
    raw_feats,
    feats,
    grads_in,
    grads_out,
    dpres,
    part_send,
    part_recv,
    stat_send,
    stat_recv,
    ws,
    wr,
    ms,
    mr,
    vs,
    vr,
    gs,
    gr,
    fs,
    fr,
    rs,
    rr,
    ps,
    pr,
    ss,
    sr,
    bs,
    br,
    ts,
    tr,
    ds,
    dr,
    local_sem,
    out_sem,
    in_sem,
):
    S, D, pr_rows, H, MB, R = sizes
    RB = S * pr_rows
    TOK = MB * R
    E = 2 * H
    s = lax.axis_index("section")
    a = lax.axis_index("dp")
    c = lax.axis_index("mp")
    sib = {"mp": 1 - c}
    lanes = H // 128
    cut = (lanes + 1) // 2 * 128
    chunks = ((0, cut), (cut, H - cut))
    width = feature_width(RB, H)
    rounds = 2 if S % 2 == 0 and RB // 2 % 16 == 0 else 1
    G, GR = S // rounds, RB // rounds
    group = s // G
    spot = lax.rem(s, G)
    groups = [group, 1 - group][:rounds]
    near = sorted(range(1, G), key=lambda k: min(k, G - k))

    barrier = pltpu.get_barrier_semaphore()

    @pl.loop(1, S)
    def _(k):
        pl.semaphore_signal(
            barrier, inc=1, device_id={"section": lax.rem(s + k, S)}, device_id_type=MESH
        )

    @pl.loop(1, D)
    def _(k):
        pl.semaphore_signal(
            barrier, inc=1, device_id={"dp": lax.rem(a + k, D)}, device_id_type=MESH
        )

    pl.semaphore_signal(barrier, inc=1, device_id=sib, device_id_type=MESH)

    loads = [
        pltpu.make_async_copy(src, dst, in_sem.at[i])
        for i, (src, dst) in enumerate(
            ((old_w_hbm, old_w), (old_m_hbm, old_m), (old_v_hbm, old_v))
        )
    ]
    for load in loads:
        load.start()

    @pl.when(s == 0)
    def _():
        @pl.loop(0, MB)
        def _(b):
            pltpu.make_async_copy(
                tokens.at[b, :, pl.ds(pl.multiple_of(c * H, 128), H)],
                acts.at[b, c],
                local_sem.at[b],
            ).start()

    @pl.when(s == S - 1)
    def _():
        @pl.loop(0, MB)
        def _(b):
            pltpu.make_async_copy(
                cotangent.at[b, :, pl.ds(pl.multiple_of(c * H, 128), H)],
                grads_in.at[b],
                local_sem.at[MB + b],
            ).start()

    loads[0].wait()

    @pl.loop(0, S)
    def _(k):
        base = order[k] * (pr_rows * lanes)
        for j in range(lanes):
            w_send[k, :, 128 * j : 128 * (j + 1)] = old_w[
                pl.ds(base + j, pr_rows, stride=lanes), :
            ].astype(BF16)

    pl.semaphore_wait(barrier, S + D - 1)

    def send_piece(send, recv, send_sems, recv_sems, to):
        remote(
            send.at[to], recv.at[s], send_sems.at[to], recv_sems.at[s], {"section": to}
        ).start()

    def peers(which, offsets):
        return [groups[which] * G + lax.rem(spot + k, G) for k in offsets]

    def arrived(send, recv, send_sems, recv_sems, which):
        for of in peers(which, near if which == 0 else range(G)):
            remote(
                send.at[of], recv.at[of], send_sems.at[of], recv_sems.at[of], {"section": of}
            ).wait_recv()

    def drained(send, recv, send_sems, recv_sems):
        @pl.loop(1, S)
        def _(k):
            of = lax.rem(s + k, S)
            remote(
                send.at[of], recv.at[of], send_sems.at[of], recv_sems.at[of], {"section": of}
            ).wait_send()

    def assemble(recv, dst, which):
        base = groups[which] * G
        rows = pl.ds(pl.multiple_of(groups[which] * GR, 16), GR)

        @pl.loop(0, lanes)
        def _(j):
            cols = pl.ds(pl.multiple_of(j * 128, 128), 128)
            for i in range(G):
                wide[pr_rows * i : pr_rows * (i + 1), :] = recv[
                    base + i, 0:pr_rows, cols
                ].astype(F32)
            dst[rows, cols] = wide[...].astype(BF16)

    for which in range(rounds):
        for to in peers(which, near if which == 0 else [0] + near):
            send_piece(w_send, w_recv, ws, wr, to)

    w_recv[s] = w_send[s]

    def rows_of(owner, r0, n):
        return weights.at[pl.ds(pl.multiple_of(owner * RB + r0, 16), n), :]

    def prepare():
        padded = pick.shape[0] // S

        @pl.loop(0, S)
        def _(k):
            shape = (padded, pr_rows * S)
            row = lax.broadcasted_iota(jnp.int32, shape, 0)
            col = lax.broadcasted_iota(jnp.int32, shape, 1)
            hit = col == row * S + order[k]
            pick[pl.ds(pl.multiple_of(k * padded, 16), padded), :] = jnp.where(
                hit & (row < pr_rows), 1.0, 0.0
            ).astype(BF16)

        def select(old, send):
            @pl.loop(0, lanes)
            def _(j):
                cols = pl.ds(pl.multiple_of(j * 128, 128), 128)
                flat = old[:, :, cols].reshape(pr_rows * S, 128)
                send[:, :, cols] = (
                    jnp.dot(pick[...], flat, preferred_element_type=F32)
                    .astype(BF16)
                    .reshape(S, padded, 128)[:, :pr_rows]
                )

        loads[1].wait()
        select(old_m, m_send)
        loads[2].wait()
        select(old_v, v_send)
        m_recv[s] = m_send[s]
        v_recv[s] = v_send[s]

    pending = []

    def begin(which):
        arrived(w_send, w_recv, ws, wr, which)
        assemble(w_recv, block, which)
        at = pl.multiple_of(groups[which] * GR, 16)
        own = pltpu.make_async_copy(
            block.at[pl.ds(at, GR), :], rows_of(a, at, GR), local_sem.at[2 * MB + which]
        )
        own.start()
        return own

    def relays(which):
        x = lax.rem(a, XS)
        h = a // XS
        base = pl.multiple_of(groups[which] * GR, 16)

        def at(dx, dh):
            hh = (1 - h) if dh else h
            return hh * XS + lax.rem(x + dx + XS, XS)

        third, half = relay_plan(GR)
        up, down, across = at(1, 0), at(-1, 0), at(0, 1)

        def start(sem, src, owner, r0, n, to):
            sem = sem + 14 * which
            cp = remote(
                src, rows_of(owner, base + r0, n), gs.at[sem], gr.at[sem], {"dp": to}
            )
            cp.start()
            pending.append(cp)

        def relay(sem, owner, r0, n, to):
            start(sem, rows_of(owner, base + r0, n), owner, r0, n, to)

        def landed(sem, owner, r0, n):
            there = rows_of(owner, base + r0, n)
            pltpu.make_async_copy(there, there, gr.at[sem + 14 * which]).wait()

        def blk(r0, n):
            return block.at[pl.ds(pl.multiple_of(base + r0, 16), n), :]

        begun = begin(which)
        start(0, blk(third, GR - third), a, third, GR - third, across)
        start(1, blk(0, third), a, 0, third, across)
        start(2, blk(0, half), a, 0, half, up)
        start(3, blk(half, GR - half), a, half, GR - half, down)
        start(4, blk(half, GR - half), a, half, GR - half, up)
        start(5, blk(0, half), a, 0, half, down)
        yield
        landed(0, across, third, GR - third)
        relay(6, across, third, GR - third, up)
        relay(7, across, third, GR - third, down)
        landed(2, down, 0, half)
        relay(8, down, 0, half, up)
        landed(3, up, half, GR - half)
        relay(9, up, half, GR - half, down)
        yield
        landed(4, down, half, GR - half)
        relay(10, down, 0, third, across)
        landed(5, up, 0, half)
        relay(11, up, 0, third, across)
        yield
        landed(1, across, 0, third)
        landed(6, at(-1, 1), third, GR - third)
        landed(10, at(-1, 1), 0, third)
        relay(12, at(-1, 1), 0, half, up)
        landed(7, at(1, 1), third, GR - third)
        landed(11, at(1, 1), 0, third)
        relay(13, at(1, 1), half, GR - half, down)
        yield
        landed(8, at(2, 0), 0, half)
        landed(9, at(2, 0), half, GR - half)
        landed(12, at(2, 1), 0, half)
        landed(13, at(2, 1), half, GR - half)
        begun.wait()
        yield

    def direct(which):
        base = pl.multiple_of(groups[which] * GR, 16)
        begun = begin(which)
        for k in range(1, D):
            to = lax.rem(a + k, D)
            sem = k + 14 * which
            cp = remote(
                block.at[pl.ds(base, GR), :],
                rows_of(a, base, GR),
                gs.at[sem],
                gr.at[sem],
                {"dp": to},
            )
            cp.start()
            pending.append(cp)
        yield
        for k in range(1, D):
            there = rows_of(lax.rem(a - k + D, D), base, GR)
            pltpu.make_async_copy(there, there, gr.at[k + 14 * which]).wait()
        begun.wait()
        for _ in range(4):
            yield

    def moments(which, offsets):
        for to in peers(which, offsets):
            send_piece(m_send, m_recv, ms, mr, to)
            send_piece(v_send, v_recv, vs, vr, to)

    routes = [(relays if D == 2 * XS else direct)(which) for which in range(rounds)]
    next(routes[0])
    prepare()
    moments(0, near)
    if rounds == 1:
        for _ in routes[0]:
            pass
    else:
        for which in (0, 1, 0, 1, 0, 1, 0, 1, 1):
            next(routes[which])

    block_copy = pltpu.make_async_copy(block, block_out, out_sem.at[0])
    block_copy.start()

    early = s < (S + 1) // 2

    def flip():
        for part_index in range(2):

            @pl.loop(0, lanes * lanes)
            def _(t):
                i = pl.multiple_of(t // lanes * 128, 128)
                j = pl.multiple_of(lax.rem(t, lanes) * 128, 128)
                flipped[part_index, pl.ds(j, 128), pl.ds(i, 128)] = jnp.transpose(
                    weights[pl.ds(pl.multiple_of(part_index * H + i, 128), 128), pl.ds(j, 128)]
                )

    behind = [0] + [k for k in near if 2 * k > G]
    ahead = [k for k in near if 2 * k <= G]
    if rounds == 2:
        moments(1, behind)

    @pl.when(jnp.logical_not(early))
    def _():
        flip()
        if rounds == 2:
            moments(1, ahead)

    gain_own = gain[c]
    gain_sib = gain[1 - c]

    def w_rows(half_index, chunk):
        at, n = chunk
        return pl.ds(pl.multiple_of(half_index * H + at, 128), n)

    @pl.loop(0, MB)
    def _(b):
        total = jnp.zeros((R, H), F32)
        square = jnp.zeros((R, 1), F32)
        own, other = [], []

        @pl.when(s == 0)
        def _():
            pltpu.make_async_copy(
                tokens.at[b, :, pl.ds(pl.multiple_of(c * H, 128), H)],
                acts.at[b, c],
                local_sem.at[b],
            ).wait()

        for q, (at, n) in enumerate(chunks):
            here = acts.at[b, c, :, pl.ds(at, n)]

            @pl.when(s > 0)
            def _():
                pltpu.make_async_copy(here, here, fr.at[b, q]).wait()

            remote(here, here, rs.at[b, q], rr.at[b, q], sib).start()
            x = acts[b, c, :, at : at + n].astype(F32)
            own.append(x)
            square = square + jnp.sum(x * x, axis=1, keepdims=True)
            total = total + jnp.dot(
                (x * gain_own[:, at : at + n]).astype(BF16),
                weights[w_rows(c, (at, n)), :],
                preferred_element_type=F32,
            )
        for q, (at, n) in enumerate(chunks):
            there = acts.at[b, 1 - c, :, pl.ds(at, n)]
            pltpu.make_async_copy(there, there, rr.at[b, q]).wait()
            x = acts[b, 1 - c, :, at : at + n].astype(F32)
            other.append(x)
            square = square + jnp.sum(x * x, axis=1, keepdims=True)
            x_gain = (x * gain_sib[:, at : at + n]).astype(BF16)
            if q == 0:
                total = total + jnp.dot(
                    x_gain, weights[w_rows(1 - c, (at, n)), :], preferred_element_type=F32
                )
        scale = lax.rsqrt(square * (1.0 / E) + eps_norm)
        for t, (to_at, to_n) in enumerate(chunks):
            pre = (
                total[:, to_at : to_at + to_n]
                + jnp.dot(
                    x_gain,
                    weights[w_rows(1 - c, chunks[1]), to_at : to_at + to_n],
                    preferred_element_type=F32,
                )
            ) * scale
            outs[b, :, to_at : to_at + to_n] = (own[t] + jax.nn.silu(pre)).astype(BF16)

            @pl.when(s < S - 1)
            def _():
                remote(
                    outs.at[b, :, pl.ds(to_at, to_n)],
                    acts.at[b, c, :, pl.ds(to_at, to_n)],
                    fs.at[b, t],
                    fr.at[b, t],
                    {"section": lax.rem(s + 1, S)},
                ).start()

            preacts[b, :, to_at : to_at + to_n] = pre
        scales[b] = jnp.broadcast_to(scale, (R, 128))
        for q, (at, n) in enumerate(chunks):
            cols = slice(at, at + n)
            normed[c, b, :, cols] = (own[q] * scale * gain_own[:, cols]).astype(BF16)
            normed[1 - c, b, :, cols] = (other[q] * scale * gain_sib[:, cols]).astype(BF16)

    per_half = H // RB

    def window(owner):
        offset = lax.rem(owner, per_half) * RB
        return owner // per_half, pl.multiple_of(offset // 128 * 128, 128)

    def send_features():
        @pl.loop(1, D)
        def _(k):
            to = lax.rem(a + k, D)
            half_index, at = window(to)
            remote(
                normed.at[half_index, :, :, pl.ds(at, width)],
                raw_feats.at[:, a],
                ts.at[to],
                tr.at[a],
                {"dp": to},
            ).start()

        half_index, at = window(a)
        raw_feats[:, a] = normed[half_index, :, :, pl.ds(at, width)]

    send_features()

    def moment_rows(recv, send, send_sems, recv_sems, dst, which):
        arrived(send, recv, send_sems, recv_sems, which)
        assemble(recv, dst, which)

    def first_rows(which):
        moment_rows(m_recv, m_send, ms, mr, first, which)

    def second_rows(which):
        moment_rows(v_recv, v_send, vs, vr, second, which)

    first_copy = pltpu.make_async_copy(first, m_out, out_sem.at[1])
    second_copy = pltpu.make_async_copy(second, v_out, out_sem.at[2])

    def near_state():
        first_rows(0)
        second_rows(0)

        @pl.loop(1, D)
        def _(k):
            of = lax.rem(a + k, D)
            pltpu.make_async_copy(raw_feats.at[:, of], raw_feats.at[:, of], tr.at[of]).wait()

        @pl.loop(0, MB)
        def _(b):
            for j in range(width // 128):
                feats[b, 128 * j : 128 * (j + 1), :] = jnp.transpose(
                    raw_feats[b, :, :, 128 * j : 128 * (j + 1)].reshape(D * R, 128)
                )

    @pl.when(early)
    def _():
        flip()
        if rounds == 2:
            moments(1, ahead)
        near_state()

    def dpre_rows(owner, b):
        return dpres.at[pl.ds(pl.multiple_of((b * D + owner) * R, R), R), :]

    my_rem = pl.multiple_of(lax.rem(lax.rem(a, per_half) * RB, 128), 16)

    def weight_grad(pair):
        @pl.loop(1, D)
        def _(k):
            of = lax.rem(a + k, D)
            for b in (2 * pair, 2 * pair + 1):
                pltpu.make_async_copy(dpre_rows(of, b), dpre_rows(of, b), dr.at[b, of]).wait()

        lhs = jnp.concatenate(
            [feats[2 * pair + i, pl.ds(my_rem, RB), :] for i in range(2)], axis=1
        )
        rows = pl.ds(pl.multiple_of(pair * 2 * D * R, 2 * D * R), 2 * D * R)

        def accumulate(cols):
            value = jnp.dot(lhs, dpres[rows, cols], preferred_element_type=F32)

            @pl.when(pair == 0)
            def _():
                grad_out[:, cols] = value

            @pl.when(pair > 0)
            def _():
                grad_out[:, cols] += value

        @pl.loop(0, H // 256)
        def _(j):
            accumulate(pl.ds(pl.multiple_of(j * 256, 128), 256))

        if H % 256:
            accumulate(pl.ds(H - H % 256, H % 256))

    @pl.loop(0, MB)
    def _(b):
        @pl.when(s == S - 1)
        def _():
            pltpu.make_async_copy(
                cotangent.at[b, :, pl.ds(pl.multiple_of(c * H, 128), H)],
                grads_in.at[b],
                local_sem.at[MB + b],
            ).wait()

        def take(q, at, n):
            here = grads_in.at[b, :, pl.ds(at, n)]

            @pl.when(s < S - 1)
            def _():
                pltpu.make_async_copy(here, here, br.at[b, q]).wait()

            upstream = grads_in[b, :, at : at + n].astype(F32)
            pre = preacts[b, :, at : at + n]
            sig = jax.nn.sigmoid(pre)
            dpre = (upstream * (sig * (1.0 + pre * (1.0 - sig)))).astype(BF16)
            dpres[pl.ds(pl.multiple_of((b * D + a) * R, R), R), at : at + n] = dpre
            return upstream, pre, dpre

        @pl.when(s == 0)
        def _():
            for q, (at, n) in enumerate(chunks):
                take(q, at, n)

        @pl.when(s > 0)
        def _():
            ups = []
            stat = jnp.zeros((R, 1), F32)
            for q, (at, n) in enumerate(chunks):
                upstream, pre, dpre = take(q, at, n)
                ups.append(upstream)
                stat = stat + jnp.sum(dpre.astype(F32) * pre, axis=1, keepdims=True)
                if q == 0:
                    away = jnp.dot(
                        dpre, flipped[1 - c, at : at + n, :], preferred_element_type=F32
                    )
                    home = jnp.dot(dpre, flipped[c, at : at + n, :], preferred_element_type=F32)
            stat_send[b] = jnp.broadcast_to(stat, (R, 128))
            remote(stat_send.at[b], stat_recv.at[b], ss.at[b], sr.at[b], sib).start()
            rows = slice(chunks[1][0], H)
            for t, (at, n) in enumerate(chunks):
                part_send[b, :, at : at + n] = (
                    away[:, at : at + n]
                    + jnp.dot(
                        dpre, flipped[1 - c, rows, at : at + n], preferred_element_type=F32
                    )
                ).astype(BF16)
                remote(
                    part_send.at[b, :, pl.ds(at, n)],
                    part_recv.at[b, :, pl.ds(at, n)],
                    ps.at[b, t],
                    pr.at[b, t],
                    sib,
                ).start()
            home = home + jnp.dot(dpre, flipped[c, rows, :], preferred_element_type=F32)
            pltpu.make_async_copy(stat_send.at[b], stat_recv.at[b], sr.at[b]).wait()
            scale = scales[b][:, :1]
            shrink = scale * scale * ((stat + stat_recv[b][:, :1]) * (1.0 / E))
            for t, (at, n) in enumerate(chunks):
                cols = slice(at, at + n)
                there = part_recv.at[b, :, pl.ds(at, n)]
                pltpu.make_async_copy(there, there, pr.at[b, t]).wait()
                dnormed = home[:, cols] + part_recv[b, :, cols].astype(F32)
                back = (
                    ups[t]
                    + scale * (gain_own[:, cols] * dnormed)
                    - acts[b, c, :, cols].astype(F32) * shrink
                )
                grads_out[b, :, cols] = back.astype(BF16)
                remote(
                    grads_out.at[b, :, pl.ds(at, n)],
                    grads_in.at[b, :, pl.ds(at, n)],
                    bs.at[b, t],
                    br.at[b, t],
                    {"section": lax.rem(s + S - 1, S)},
                ).start()

        @pl.loop(1, D)
        def _(k):
            to = lax.rem(a + k, D)
            remote(
                dpre_rows(a, b), dpre_rows(a, b), ds.at[b, to], dr.at[b, a], {"dp": to}
            ).start()

        @pl.when((s == 0) & (b >= 3) & (lax.rem(b, 2) == 1))
        def _():
            weight_grad((b - 3) // 2)

        @pl.when((s == 0) & (b == MB - 4))
        def _():
            if rounds == 2:
                first_rows(1)
            first_copy.start()

        @pl.when((s == 0) & (b == MB - 2))
        def _():
            if rounds == 2:
                second_rows(1)
            second_copy.start()

    @pl.when(jnp.logical_not(early))
    def _():
        near_state()

    @pl.when(s > 0)
    def _():
        if rounds == 2:
            first_rows(1)
            second_rows(1)
        first_copy.start()
        second_copy.start()

    @pl.loop(jnp.where(s == 0, MB // 2 - 1, 0), MB // 2)
    def _(pair):
        weight_grad(pair)

    block_copy.wait()
    first_copy.wait()
    second_copy.wait()
    drained(w_send, w_recv, ws, wr)
    drained(m_send, m_recv, ms, mr)
    drained(v_send, v_recv, vs, vr)
    for cp in pending:
        cp.wait_send()

    @pl.loop(0, MB)
    def _(b):
        for q, (at, n) in enumerate(chunks):
            here = acts.at[b, c, :, pl.ds(at, n)]
            remote(here, here, rs.at[b, q], rr.at[b, q], sib).wait_send()

            @pl.when(s < S - 1)
            def _():
                out = outs.at[b, :, pl.ds(at, n)]
                remote(out, here, fs.at[b, q], fr.at[b, q], sib).wait_send()

            @pl.when(s > 0)
            def _():
                part = part_send.at[b, :, pl.ds(at, n)]
                remote(
                    part, part_recv.at[b, :, pl.ds(at, n)], ps.at[b, q], pr.at[b, q], sib
                ).wait_send()
                back = grads_out.at[b, :, pl.ds(at, n)]
                remote(
                    back, grads_in.at[b, :, pl.ds(at, n)], bs.at[b, q], br.at[b, q], sib
                ).wait_send()

        @pl.when(s > 0)
        def _():
            remote(stat_send.at[b], stat_recv.at[b], ss.at[b], sr.at[b], sib).wait_send()

        @pl.loop(1, D)
        def _(k):
            to = lax.rem(a + k, D)
            remote(
                dpre_rows(a, b), dpre_rows(a, b), ds.at[b, to], dr.at[b, a], {"dp": to}
            ).wait_send()

    @pl.loop(1, D)
    def _(k):
        to = lax.rem(a + k, D)
        half_index, at = window(to)
        remote(
            normed.at[half_index, :, :, pl.ds(at, width)],
            raw_feats.at[:, a],
            ts.at[to],
            tr.at[a],
            {"dp": to},
        ).wait_send()


def local(old_w, old_m, old_v, old_slot_layer, norm_gain, tokens, cotangent):
    S = lax.axis_size("section")
    D = lax.axis_size("dp")
    PR, H = old_w.shape[3], old_w.shape[4]
    MB, R = tokens.shape[0], tokens.shape[1]
    RB = S * PR
    TOK = MB * R
    E = 2 * H
    layer_ids = jnp.arange(S, dtype=jnp.int32)
    matches = (old_slot_layer[None, :] == layer_ids[:, None]).astype(jnp.int32)
    order = jnp.sum(matches * layer_ids[None, :], axis=1)
    vmem = pl.BlockSpec(memory_space=pltpu.VMEM)
    anyspace = pl.BlockSpec(memory_space=pl.ANY)
    dma = pltpu.SemaphoreType.DMA
    padded = -(-PR // 16) * 16
    group_rows = RB // 2 if S % 2 == 0 and RB // 2 % 16 == 0 else RB
    width = feature_width(RB, H)
    grad, master, moment, square = pl.pallas_call(
        functools.partial(kernel, (S, D, PR, H, MB, R)),
        out_shape=(
            jax.ShapeDtypeStruct((RB, H), F32),
            jax.ShapeDtypeStruct((RB, H), BF16),
            jax.ShapeDtypeStruct((RB, H), BF16),
            jax.ShapeDtypeStruct((RB, H), BF16),
        ),
        in_specs=[pl.BlockSpec(memory_space=pltpu.SMEM), anyspace, anyspace, anyspace, vmem, anyspace, anyspace],
        out_specs=(vmem, anyspace, anyspace, anyspace),
        scratch_shapes=[
            pltpu.VMEM((S * PR * H // 128, 128), F32),
            pltpu.VMEM((PR, S, H), BF16),
            pltpu.VMEM((PR, S, H), BF16),
            pltpu.VMEM((S, PR, H), BF16),
            pltpu.VMEM((S, PR, H), BF16),
            pltpu.VMEM((S, PR, H), BF16),
            pltpu.VMEM((S, PR, H), BF16),
            pltpu.VMEM((S, PR, H), BF16),
            pltpu.VMEM((S, PR, H), BF16),
            pltpu.VMEM((S * padded, PR * S), BF16),
            pltpu.VMEM((group_rows, 128), F32),
            pltpu.VMEM((RB, H), BF16),
            pltpu.VMEM((RB, H), BF16),
            pltpu.VMEM((RB, H), BF16),
            pltpu.VMEM((E, H), BF16),
            pltpu.VMEM((2, H, H), BF16),
            pltpu.VMEM((MB, 2, R, H), BF16),
            pltpu.VMEM((MB, R, H), BF16),
            pltpu.VMEM((MB, R, H), F32),
            pltpu.VMEM((MB, R, 128), F32),
            pltpu.VMEM((2, MB, R, H), BF16),
            pltpu.VMEM((MB, D, R, width), BF16),
            pltpu.VMEM((MB, width, D * R), BF16),
            pltpu.VMEM((MB, R, H), BF16),
            pltpu.VMEM((MB, R, H), BF16),
            pltpu.VMEM((D * TOK, H), BF16),
            pltpu.VMEM((MB, R, H), BF16),
            pltpu.VMEM((MB, R, H), BF16),
            pltpu.VMEM((MB, R, 128), F32),
            pltpu.VMEM((MB, R, 128), F32),
            dma((S,)),
            dma((S,)),
            dma((S,)),
            dma((S,)),
            dma((S,)),
            dma((S,)),
            dma((28,)),
            dma((28,)),
            dma((MB, 2)),
            dma((MB, 2)),
            dma((MB, 2)),
            dma((MB, 2)),
            dma((MB, 2)),
            dma((MB, 2)),
            dma((MB,)),
            dma((MB,)),
            dma((MB, 2)),
            dma((MB, 2)),
            dma((D,)),
            dma((D,)),
            dma((MB, D)),
            dma((MB, D)),
            dma((2 * MB + 2,)),
            dma((3,)),
            dma((3,)),
        ],
        compiler_params=pltpu.CompilerParams(
            collective_id=0, has_side_effects=True, vmem_limit_bytes=63_000_000
        ),
    )(
        order,
        old_w.reshape(S * PR * H // 128, 128),
        old_m.reshape(S, PR, H).transpose(1, 0, 2),
        old_v.reshape(S, PR, H).transpose(1, 0, 2),
        norm_gain.reshape(2, 1, H),
        tokens,
        cotangent,
    )
    moment_next = beta_one * moment.astype(F32) + (1.0 - beta_one) * grad
    second_next = beta_two * square.astype(F32) + (1.0 - beta_two) * grad * grad
    fix_one = 1.0 - beta_one**step_count
    fix_two = 1.0 - beta_two**step_count
    direction = moment_next / fix_one / (jnp.sqrt(second_next / fix_two) + adam_eps)
    kept = master.astype(F32)
    updated = kept - learn_rate * (direction + decay_rate * kept)
    return updated[None], moment_next.astype(BF16)[None], second_next.astype(BF16)[None]


def solution(mesh):
    placed = (
        P(None, "dp", "section", None, "mp"),
        P(None, "dp", "section", None, "mp"),
        P(None, "dp", "section", None, "mp"),
        P(),
        P("section", None),
        P(None, "dp", None),
        P(None, "dp", None),
    )
    return jax.shard_map(
        local,
        mesh=mesh,
        in_specs=placed,
        out_specs=(P("section", "dp", "mp"), P("section", "dp", "mp"), P("section", "dp", "mp")),
        check_vma=False,
    )
```

```python
import functools

import jax
import jax.numpy as jnp
from jax import lax
from jax.experimental import pallas as pl
from jax.experimental.pallas import tpu as pltpu
from jax.sharding import PartitionSpec as P

eps_norm = 1e-05
beta_one = 0.9
beta_two = 0.95
learn_rate = 0.001
decay_rate = 0.1
adam_eps = 1e-08
step_count = 1000.0

MESH = pl.DeviceIdType.MESH
F32 = jnp.float32
BF16 = jnp.bfloat16
XS = 4


def remote(src, dst, send_sem, recv_sem, device):
    return pltpu.make_async_remote_copy(
        src_ref=src,
        dst_ref=dst,
        send_sem=send_sem,
        recv_sem=recv_sem,
        device_id=device,
        device_id_type=MESH,
    )


def relay_plan(rows):
    two_thirds = max(16, (rows * 2 // 3 + 15) // 16 * 16)
    half = (rows // 2 + 15) // 16 * 16
    return two_thirds, half


def feature_width(rows, half):
    return max(
        -(-(rows * k % 128 + rows) // 128) * 128 for k in range(half // rows)
    )


def kernel(
    sizes,
    slot_layer,
    old_w_hbm,
    old_m_hbm,
    old_v_hbm,
    gain,
    tokens,
    cotangent,
    grad_out,
    block_out,
    m_out,
    v_out,
    old_w,
    old_m,
    old_v,
    w_send,
    m_send,
    v_send,
    w_recv,
    m_recv,
    v_recv,
    pick,
    wide,
    block,
    first,
    second,
    weights,
    flipped,
    acts,
    outs,
    preacts,
    scales,
    normed,
    raw_feats,
    feats,
    grads_in,
    grads_out,
    dpres,
    part_send,
    part_recv,
    stat_send,
    stat_recv,
    ws,
    wr,
    ms,
    mr,
    vs,
    vr,
    gs,
    gr,
    fs,
    fr,
    rs,
    rr,
    ps,
    pr,
    ss,
    sr,
    bs,
    br,
    ts,
    tr,
    ds,
    dr,
    local_sem,
    out_sem,
    in_sem,
):
    S, D, pr_rows, H, MB, R = sizes
    RB = S * pr_rows
    TOK = MB * R
    E = 2 * H
    s = lax.axis_index("section")
    a = lax.axis_index("dp")
    c = lax.axis_index("mp")
    sib = {"mp": 1 - c}
    lanes = H // 128
    cut = (lanes + 1) // 2 * 128
    chunks = ((0, cut), (cut, H - cut))
    width = feature_width(RB, H)
    rounds = 2 if S % 2 == 0 and RB // 2 % 16 == 0 else 1
    G, GR = S // rounds, RB // rounds
    group = s // G
    spot = lax.rem(s, G)
    groups = [group, 1 - group][:rounds]
    near = sorted(range(1, G), key=lambda k: min(k, G - k))

    barrier = pltpu.get_barrier_semaphore()

    @pl.loop(1, S)
    def _(k):
        pl.semaphore_signal(
            barrier, inc=1, device_id={"section": lax.rem(s + k, S)}, device_id_type=MESH
        )

    @pl.loop(1, D)
    def _(k):
        pl.semaphore_signal(
            barrier, inc=1, device_id={"dp": lax.rem(a + k, D)}, device_id_type=MESH
        )

    pl.semaphore_signal(barrier, inc=1, device_id=sib, device_id_type=MESH)

    loads = [
        pltpu.make_async_copy(src, dst, in_sem.at[i])
        for i, (src, dst) in enumerate(
            ((old_w_hbm, old_w), (old_m_hbm, old_m), (old_v_hbm, old_v))
        )
    ]
    for load in loads:
        load.start()

    @pl.when(s == 0)
    def _():
        @pl.loop(0, MB)
        def _(b):
            pltpu.make_async_copy(
                tokens.at[b, :, pl.ds(pl.multiple_of(c * H, 128), H)],
                acts.at[b, c],
                local_sem.at[b],
            ).start()

    @pl.when(s == S - 1)
    def _():
        @pl.loop(0, MB)
        def _(b):
            pltpu.make_async_copy(
                cotangent.at[b, :, pl.ds(pl.multiple_of(c * H, 128), H)],
                grads_in.at[b],
                local_sem.at[MB + b],
            ).start()

    loads[0].wait()

    def slot_of(layer):
        slot = jnp.int32(0)
        for j in range(1, S):
            slot = jnp.where(slot_layer[j] == layer, j, slot)
        return slot

    @pl.loop(0, S)
    def _(k):
        base = slot_of(k) * (pr_rows * lanes)
        for j in range(lanes):
            w_send[k, :, 128 * j : 128 * (j + 1)] = old_w[
                pl.ds(base + j, pr_rows, stride=lanes), :
            ].astype(BF16)

    pl.semaphore_wait(barrier, S + D - 1)

    def send_piece(send, recv, send_sems, recv_sems, to):
        remote(
            send.at[to], recv.at[s], send_sems.at[to], recv_sems.at[s], {"section": to}
        ).start()

    def peers(which, offsets):
        return [groups[which] * G + lax.rem(spot + k, G) for k in offsets]

    def arrived(send, recv, send_sems, recv_sems, which):
        for of in peers(which, near if which == 0 else range(G)):
            remote(
                send.at[of], recv.at[of], send_sems.at[of], recv_sems.at[of], {"section": of}
            ).wait_recv()

    def drained(send, recv, send_sems, recv_sems):
        @pl.loop(1, S)
        def _(k):
            of = lax.rem(s + k, S)
            remote(
                send.at[of], recv.at[of], send_sems.at[of], recv_sems.at[of], {"section": of}
            ).wait_send()

    def assemble(recv, dst, which):
        base = groups[which] * G
        rows = pl.ds(pl.multiple_of(groups[which] * GR, 16), GR)

        @pl.loop(0, lanes)
        def _(j):
            cols = pl.ds(pl.multiple_of(j * 128, 128), 128)
            for i in range(G):
                wide[pr_rows * i : pr_rows * (i + 1), :] = recv[
                    base + i, 0:pr_rows, cols
                ].astype(F32)
            dst[rows, cols] = wide[...].astype(BF16)

    @pl.loop(0, S)
    def _(k):
        to = lax.rem(k, rounds) * G + k // rounds

        @pl.when(to != s)
        def _():
            send_piece(w_send, w_recv, ws, wr, to)

    w_recv[s] = w_send[s]

    def rows_of(owner, r0, n):
        return weights.at[pl.ds(pl.multiple_of(owner * RB + r0, 16), n), :]

    def prepare():
        padded = pick.shape[0] // S

        @pl.loop(0, S)
        def _(k):
            shape = (padded, pr_rows * S)
            row = lax.broadcasted_iota(jnp.int32, shape, 0)
            col = lax.broadcasted_iota(jnp.int32, shape, 1)
            hit = col == row * S + slot_of(k)
            pick[pl.ds(pl.multiple_of(k * padded, 16), padded), :] = jnp.where(
                hit & (row < pr_rows), 1.0, 0.0
            ).astype(BF16)

        def select(old, send):
            @pl.loop(0, lanes)
            def _(j):
                cols = pl.ds(pl.multiple_of(j * 128, 128), 128)
                flat = old[:, :, cols].reshape(pr_rows * S, 128)
                send[:, :, cols] = (
                    jnp.dot(pick[...], flat, preferred_element_type=F32)
                    .astype(BF16)
                    .reshape(S, padded, 128)[:, :pr_rows]
                )

        loads[1].wait()
        select(old_m, m_send)
        loads[2].wait()
        select(old_v, v_send)
        m_recv[s] = m_send[s]
        v_recv[s] = v_send[s]

    pending = []

    def begin(which):
        arrived(w_send, w_recv, ws, wr, which)
        assemble(w_recv, block, which)
        at = pl.multiple_of(groups[which] * GR, 16)
        own = pltpu.make_async_copy(
            block.at[pl.ds(at, GR), :], rows_of(a, at, GR), local_sem.at[2 * MB + which]
        )
        own.start()
        return own

    def relays(which):
        x = lax.rem(a, XS)
        h = a // XS
        base = pl.multiple_of(groups[which] * GR, 16)

        def at(dx, dh):
            hh = (1 - h) if dh else h
            return hh * XS + lax.rem(x + dx + XS, XS)

        third, half = relay_plan(GR)
        up, down, across = at(1, 0), at(-1, 0), at(0, 1)

        def start(sem, src, owner, r0, n, to):
            sem = sem + 14 * which
            cp = remote(
                src, rows_of(owner, base + r0, n), gs.at[sem], gr.at[sem], {"dp": to}
            )
            cp.start()
            pending.append(cp)

        def relay(sem, owner, r0, n, to):
            start(sem, rows_of(owner, base + r0, n), owner, r0, n, to)

        def landed(sem, owner, r0, n):
            there = rows_of(owner, base + r0, n)
            pltpu.make_async_copy(there, there, gr.at[sem + 14 * which]).wait()

        def blk(r0, n):
            return block.at[pl.ds(pl.multiple_of(base + r0, 16), n), :]

        begun = begin(which)
        start(0, blk(third, GR - third), a, third, GR - third, across)
        start(1, blk(0, third), a, 0, third, across)
        start(2, blk(0, half), a, 0, half, up)
        start(3, blk(half, GR - half), a, half, GR - half, down)
        start(4, blk(half, GR - half), a, half, GR - half, up)
        start(5, blk(0, half), a, 0, half, down)
        yield
        landed(0, across, third, GR - third)
        relay(6, across, third, GR - third, up)
        relay(7, across, third, GR - third, down)
        landed(2, down, 0, half)
        relay(8, down, 0, half, up)
        landed(3, up, half, GR - half)
        relay(9, up, half, GR - half, down)
        yield
        landed(4, down, half, GR - half)
        relay(10, down, 0, third, across)
        landed(5, up, 0, half)
        relay(11, up, 0, third, across)
        yield
        landed(1, across, 0, third)
        landed(6, at(-1, 1), third, GR - third)
        landed(10, at(-1, 1), 0, third)
        relay(12, at(-1, 1), 0, half, up)
        landed(7, at(1, 1), third, GR - third)
        landed(11, at(1, 1), 0, third)
        relay(13, at(1, 1), half, GR - half, down)
        yield
        landed(8, at(2, 0), 0, half)
        landed(9, at(2, 0), half, GR - half)
        landed(12, at(2, 1), 0, half)
        landed(13, at(2, 1), half, GR - half)
        begun.wait()
        yield

    def direct(which):
        base = pl.multiple_of(groups[which] * GR, 16)
        begun = begin(which)
        for k in range(1, D):
            to = lax.rem(a + k, D)
            sem = k + 14 * which
            cp = remote(
                block.at[pl.ds(base, GR), :],
                rows_of(a, base, GR),
                gs.at[sem],
                gr.at[sem],
                {"dp": to},
            )
            cp.start()
            pending.append(cp)
        yield
        for k in range(1, D):
            there = rows_of(lax.rem(a - k + D, D), base, GR)
            pltpu.make_async_copy(there, there, gr.at[k + 14 * which]).wait()
        begun.wait()
        for _ in range(4):
            yield

    def moments(which, offsets):
        for to in peers(which, offsets):
            send_piece(m_send, m_recv, ms, mr, to)
            send_piece(v_send, v_recv, vs, vr, to)

    routes = [(relays if D == 2 * XS else direct)(which) for which in range(rounds)]
    next(routes[0])
    prepare()
    moments(0, near)
    if rounds == 1:
        for _ in routes[0]:
            pass
    else:
        for which in (0, 0, 1, 0, 1, 1, 1, 0, 1):
            next(routes[which])

    block_copy = pltpu.make_async_copy(block, block_out, out_sem.at[0])
    block_copy.start()

    early = s < (S + 1) // 2

    def flip():
        for part_index in range(2):

            @pl.loop(0, lanes * lanes)
            def _(t):
                i = pl.multiple_of(t // lanes * 128, 128)
                j = pl.multiple_of(lax.rem(t, lanes) * 128, 128)
                flipped[part_index, pl.ds(j, 128), pl.ds(i, 128)] = jnp.transpose(
                    weights[pl.ds(pl.multiple_of(part_index * H + i, 128), 128), pl.ds(j, 128)]
                )

    behind = [0] + [k for k in near if 2 * k > G]
    ahead = [k for k in near if 2 * k <= G]
    if rounds == 2:
        moments(1, behind)

    @pl.when(jnp.logical_not(early))
    def _():
        flip()

    gain_own = gain[c]
    gain_sib = gain[1 - c]

    def w_rows(half_index, chunk):
        at, n = chunk
        return pl.ds(pl.multiple_of(half_index * H + at, 128), n)

    @pl.loop(0, MB)
    def _(b):
        total = jnp.zeros((R, H), F32)
        square = jnp.zeros((R, 1), F32)
        own, other = [], []

        @pl.when(s == 0)
        def _():
            pltpu.make_async_copy(
                tokens.at[b, :, pl.ds(pl.multiple_of(c * H, 128), H)],
                acts.at[b, c],
                local_sem.at[b],
            ).wait()

        for q, (at, n) in enumerate(chunks):
            here = acts.at[b, c, :, pl.ds(at, n)]

            @pl.when(s > 0)
            def _():
                pltpu.make_async_copy(here, here, fr.at[b, q]).wait()

            remote(here, here, rs.at[b, q], rr.at[b, q], sib).start()
            x = acts[b, c, :, at : at + n].astype(F32)
            own.append(x)
            square = square + jnp.sum(x * x, axis=1, keepdims=True)
            total = total + jnp.dot(
                (x * gain_own[:, at : at + n]).astype(BF16),
                weights[w_rows(c, (at, n)), :],
                preferred_element_type=F32,
            )
        for q, (at, n) in enumerate(chunks):
            there = acts.at[b, 1 - c, :, pl.ds(at, n)]
            pltpu.make_async_copy(there, there, rr.at[b, q]).wait()
            x = acts[b, 1 - c, :, at : at + n].astype(F32)
            other.append(x)
            square = square + jnp.sum(x * x, axis=1, keepdims=True)
            x_gain = (x * gain_sib[:, at : at + n]).astype(BF16)
            if q == 0:
                total = total + jnp.dot(
                    x_gain, weights[w_rows(1 - c, (at, n)), :], preferred_element_type=F32
                )
        scale = lax.rsqrt(square * (1.0 / E) + eps_norm)
        for t, (to_at, to_n) in enumerate(chunks):
            pre = (
                total[:, to_at : to_at + to_n]
                + jnp.dot(
                    x_gain,
                    weights[w_rows(1 - c, chunks[1]), to_at : to_at + to_n],
                    preferred_element_type=F32,
                )
            ) * scale
            outs[b, :, to_at : to_at + to_n] = (own[t] + jax.nn.silu(pre)).astype(BF16)

            @pl.when(s < S - 1)
            def _():
                remote(
                    outs.at[b, :, pl.ds(to_at, to_n)],
                    acts.at[b, c, :, pl.ds(to_at, to_n)],
                    fs.at[b, t],
                    fr.at[b, t],
                    {"section": lax.rem(s + 1, S)},
                ).start()

            preacts[b, :, to_at : to_at + to_n] = pre
        scales[b] = jnp.broadcast_to(scale, (R, 128))
        for q, (at, n) in enumerate(chunks):
            cols = slice(at, at + n)
            normed[c, b, :, cols] = (own[q] * scale * gain_own[:, cols]).astype(BF16)
            normed[1 - c, b, :, cols] = (other[q] * scale * gain_sib[:, cols]).astype(BF16)

    per_half = H // RB

    def window(owner):
        offset = lax.rem(owner, per_half) * RB
        return owner // per_half, pl.multiple_of(offset // 128 * 128, 128)

    def send_features():
        @pl.loop(1, D)
        def _(k):
            to = lax.rem(a + k, D)
            half_index, at = window(to)
            remote(
                normed.at[half_index, :, :, pl.ds(at, width)],
                raw_feats.at[:, a],
                ts.at[to],
                tr.at[a],
                {"dp": to},
            ).start()

        half_index, at = window(a)
        raw_feats[:, a] = normed[half_index, :, :, pl.ds(at, width)]

    send_features()

    def moment_rows(recv, send, send_sems, recv_sems, dst, which):
        arrived(send, recv, send_sems, recv_sems, which)
        assemble(recv, dst, which)

    def first_rows(which):
        moment_rows(m_recv, m_send, ms, mr, first, which)

    def second_rows(which):
        moment_rows(v_recv, v_send, vs, vr, second, which)

    first_copy = pltpu.make_async_copy(first, m_out, out_sem.at[1])
    second_copy = pltpu.make_async_copy(second, v_out, out_sem.at[2])

    def near_state():
        first_rows(0)
        second_rows(0)

        @pl.loop(1, D)
        def _(k):
            of = lax.rem(a + k, D)
            pltpu.make_async_copy(raw_feats.at[:, of], raw_feats.at[:, of], tr.at[of]).wait()

        @pl.loop(0, MB)
        def _(b):
            for j in range(width // 128):
                feats[b, 128 * j : 128 * (j + 1), :] = jnp.transpose(
                    raw_feats[b, :, :, 128 * j : 128 * (j + 1)].reshape(D * R, 128)
                )

    @pl.when(early)
    def _():
        flip()
        near_state()

    def dpre_rows(owner, b):
        return dpres.at[pl.ds(pl.multiple_of((b * D + owner) * R, R), R), :]

    my_rem = pl.multiple_of(lax.rem(lax.rem(a, per_half) * RB, 128), 16)

    def weight_grad(pair):
        @pl.loop(1, D)
        def _(k):
            of = lax.rem(a + k, D)
            for b in (2 * pair, 2 * pair + 1):
                pltpu.make_async_copy(dpre_rows(of, b), dpre_rows(of, b), dr.at[b, of]).wait()

        lhs = jnp.concatenate(
            [feats[2 * pair + i, pl.ds(my_rem, RB), :] for i in range(2)], axis=1
        )
        rows = pl.ds(pl.multiple_of(pair * 2 * D * R, 2 * D * R), 2 * D * R)

        def accumulate(cols):
            value = jnp.dot(lhs, dpres[rows, cols], preferred_element_type=F32)

            @pl.when(pair == 0)
            def _():
                grad_out[:, cols] = value

            @pl.when(pair > 0)
            def _():
                grad_out[:, cols] += value

        @pl.loop(0, H // 256)
        def _(j):
            accumulate(pl.ds(pl.multiple_of(j * 256, 128), 256))

        if H % 256:
            accumulate(pl.ds(H - H % 256, H % 256))

    @pl.loop(0, MB)
    def _(b):
        @pl.when(s == S - 1)
        def _():
            pltpu.make_async_copy(
                cotangent.at[b, :, pl.ds(pl.multiple_of(c * H, 128), H)],
                grads_in.at[b],
                local_sem.at[MB + b],
            ).wait()

        def take(q, at, n):
            here = grads_in.at[b, :, pl.ds(at, n)]

            @pl.when(s < S - 1)
            def _():
                pltpu.make_async_copy(here, here, br.at[b, q]).wait()

            upstream = grads_in[b, :, at : at + n].astype(F32)
            pre = preacts[b, :, at : at + n]
            sig = jax.nn.sigmoid(pre)
            dpre = (upstream * (sig * (1.0 + pre * (1.0 - sig)))).astype(BF16)
            dpres[pl.ds(pl.multiple_of((b * D + a) * R, R), R), at : at + n] = dpre
            return upstream, pre, dpre

        @pl.when(s == 0)
        def _():
            for q, (at, n) in enumerate(chunks):
                take(q, at, n)

        @pl.when(s > 0)
        def _():
            ups = []
            stat = jnp.zeros((R, 1), F32)
            for q, (at, n) in enumerate(chunks):
                upstream, pre, dpre = take(q, at, n)
                ups.append(upstream)
                stat = stat + jnp.sum(dpre.astype(F32) * pre, axis=1, keepdims=True)
                if q == 0:
                    away = jnp.dot(
                        dpre, flipped[1 - c, at : at + n, :], preferred_element_type=F32
                    )
                    home = jnp.dot(dpre, flipped[c, at : at + n, :], preferred_element_type=F32)
            stat_send[b] = jnp.broadcast_to(stat, (R, 128))
            remote(stat_send.at[b], stat_recv.at[b], ss.at[b], sr.at[b], sib).start()
            rows = slice(chunks[1][0], H)
            for t, (at, n) in enumerate(chunks):
                part_send[b, :, at : at + n] = (
                    away[:, at : at + n]
                    + jnp.dot(
                        dpre, flipped[1 - c, rows, at : at + n], preferred_element_type=F32
                    )
                ).astype(BF16)
                remote(
                    part_send.at[b, :, pl.ds(at, n)],
                    part_recv.at[b, :, pl.ds(at, n)],
                    ps.at[b, t],
                    pr.at[b, t],
                    sib,
                ).start()
            home = home + jnp.dot(dpre, flipped[c, rows, :], preferred_element_type=F32)
            pltpu.make_async_copy(stat_send.at[b], stat_recv.at[b], sr.at[b]).wait()
            scale = scales[b][:, :1]
            shrink = scale * scale * ((stat + stat_recv[b][:, :1]) * (1.0 / E))
            for t, (at, n) in enumerate(chunks):
                cols = slice(at, at + n)
                there = part_recv.at[b, :, pl.ds(at, n)]
                pltpu.make_async_copy(there, there, pr.at[b, t]).wait()
                dnormed = home[:, cols] + part_recv[b, :, cols].astype(F32)
                back = (
                    ups[t]
                    + scale * (gain_own[:, cols] * dnormed)
                    - acts[b, c, :, cols].astype(F32) * shrink
                )
                grads_out[b, :, cols] = back.astype(BF16)
                remote(
                    grads_out.at[b, :, pl.ds(at, n)],
                    grads_in.at[b, :, pl.ds(at, n)],
                    bs.at[b, t],
                    br.at[b, t],
                    {"section": lax.rem(s + S - 1, S)},
                ).start()

        @pl.loop(1, D)
        def _(k):
            to = lax.rem(a + k, D)
            remote(
                dpre_rows(a, b), dpre_rows(a, b), ds.at[b, to], dr.at[b, a], {"dp": to}
            ).start()

        if rounds == 2:

            @pl.when(b == 0)
            def _():
                moments(1, ahead)

        @pl.when((s == 0) & (b >= 3) & (lax.rem(b, 2) == 1))
        def _():
            weight_grad((b - 3) // 2)

        @pl.when((s == 0) & (b == MB - 4))
        def _():
            if rounds == 2:
                first_rows(1)
            first_copy.start()

        @pl.when((s == 0) & (b == MB - 2))
        def _():
            if rounds == 2:
                second_rows(1)
            second_copy.start()

    @pl.when(jnp.logical_not(early))
    def _():
        near_state()

    @pl.when(s > 0)
    def _():
        if rounds == 2:
            first_rows(1)
            second_rows(1)
        first_copy.start()
        second_copy.start()

    @pl.loop(jnp.where(s == 0, MB // 2 - 1, 0), MB // 2)
    def _(pair):
        weight_grad(pair)

    block_copy.wait()
    first_copy.wait()
    second_copy.wait()
    drained(w_send, w_recv, ws, wr)
    drained(m_send, m_recv, ms, mr)
    drained(v_send, v_recv, vs, vr)
    for cp in pending:
        cp.wait_send()

    @pl.loop(0, MB)
    def _(b):
        for q, (at, n) in enumerate(chunks):
            here = acts.at[b, c, :, pl.ds(at, n)]
            remote(here, here, rs.at[b, q], rr.at[b, q], sib).wait_send()

            @pl.when(s < S - 1)
            def _():
                out = outs.at[b, :, pl.ds(at, n)]
                remote(out, here, fs.at[b, q], fr.at[b, q], sib).wait_send()

            @pl.when(s > 0)
            def _():
                part = part_send.at[b, :, pl.ds(at, n)]
                remote(
                    part, part_recv.at[b, :, pl.ds(at, n)], ps.at[b, q], pr.at[b, q], sib
                ).wait_send()
                back = grads_out.at[b, :, pl.ds(at, n)]
                remote(
                    back, grads_in.at[b, :, pl.ds(at, n)], bs.at[b, q], br.at[b, q], sib
                ).wait_send()

        @pl.when(s > 0)
        def _():
            remote(stat_send.at[b], stat_recv.at[b], ss.at[b], sr.at[b], sib).wait_send()

        @pl.loop(1, D)
        def _(k):
            to = lax.rem(a + k, D)
            remote(
                dpre_rows(a, b), dpre_rows(a, b), ds.at[b, to], dr.at[b, a], {"dp": to}
            ).wait_send()

    @pl.loop(1, D)
    def _(k):
        to = lax.rem(a + k, D)
        half_index, at = window(to)
        remote(
            normed.at[half_index, :, :, pl.ds(at, width)],
            raw_feats.at[:, a],
            ts.at[to],
            tr.at[a],
            {"dp": to},
        ).wait_send()


def local(old_w, old_m, old_v, old_slot_layer, norm_gain, tokens, cotangent):
    S = lax.axis_size("section")
    D = lax.axis_size("dp")
    PR, H = old_w.shape[3], old_w.shape[4]
    MB, R = tokens.shape[0], tokens.shape[1]
    RB = S * PR
    TOK = MB * R
    E = 2 * H
    vmem = pl.BlockSpec(memory_space=pltpu.VMEM)
    anyspace = pl.BlockSpec(memory_space=pl.ANY)
    dma = pltpu.SemaphoreType.DMA
    padded = -(-PR // 16) * 16
    group_rows = RB // 2 if S % 2 == 0 and RB // 2 % 16 == 0 else RB
    width = feature_width(RB, H)
    grad, master, moment, square = pl.pallas_call(
        functools.partial(kernel, (S, D, PR, H, MB, R)),
        out_shape=(
            jax.ShapeDtypeStruct((RB, H), F32),
            jax.ShapeDtypeStruct((RB, H), BF16),
            jax.ShapeDtypeStruct((RB, H), BF16),
            jax.ShapeDtypeStruct((RB, H), BF16),
        ),
        in_specs=[pl.BlockSpec(memory_space=pltpu.SMEM), anyspace, anyspace, anyspace, vmem, anyspace, anyspace],
        out_specs=(vmem, anyspace, anyspace, anyspace),
        scratch_shapes=[
            pltpu.VMEM((S * PR * H // 128, 128), F32),
            pltpu.VMEM((PR, S, H), BF16),
            pltpu.VMEM((PR, S, H), BF16),
            pltpu.VMEM((S, PR, H), BF16),
            pltpu.VMEM((S, PR, H), BF16),
            pltpu.VMEM((S, PR, H), BF16),
            pltpu.VMEM((S, PR, H), BF16),
            pltpu.VMEM((S, PR, H), BF16),
            pltpu.VMEM((S, PR, H), BF16),
            pltpu.VMEM((S * padded, PR * S), BF16),
            pltpu.VMEM((group_rows, 128), F32),
            pltpu.VMEM((RB, H), BF16),
            pltpu.VMEM((RB, H), BF16),
            pltpu.VMEM((RB, H), BF16),
            pltpu.VMEM((E, H), BF16),
            pltpu.VMEM((2, H, H), BF16),
            pltpu.VMEM((MB, 2, R, H), BF16),
            pltpu.VMEM((MB, R, H), BF16),
            pltpu.VMEM((MB, R, H), F32),
            pltpu.VMEM((MB, R, 128), F32),
            pltpu.VMEM((2, MB, R, H), BF16),
            pltpu.VMEM((MB, D, R, width), BF16),
            pltpu.VMEM((MB, width, D * R), BF16),
            pltpu.VMEM((MB, R, H), BF16),
            pltpu.VMEM((MB, R, H), BF16),
            pltpu.VMEM((D * TOK, H), BF16),
            pltpu.VMEM((MB, R, H), BF16),
            pltpu.VMEM((MB, R, H), BF16),
            pltpu.VMEM((MB, R, 128), F32),
            pltpu.VMEM((MB, R, 128), F32),
            dma((S,)),
            dma((S,)),
            dma((S,)),
            dma((S,)),
            dma((S,)),
            dma((S,)),
            dma((28,)),
            dma((28,)),
            dma((MB, 2)),
            dma((MB, 2)),
            dma((MB, 2)),
            dma((MB, 2)),
            dma((MB, 2)),
            dma((MB, 2)),
            dma((MB,)),
            dma((MB,)),
            dma((MB, 2)),
            dma((MB, 2)),
            dma((D,)),
            dma((D,)),
            dma((MB, D)),
            dma((MB, D)),
            dma((2 * MB + 2,)),
            dma((3,)),
            dma((3,)),
        ],
        compiler_params=pltpu.CompilerParams(
            collective_id=0, has_side_effects=True, vmem_limit_bytes=63_000_000
        ),
    )(
        old_slot_layer,
        old_w.reshape(S * PR * H // 128, 128),
        old_m.reshape(S, PR, H).transpose(1, 0, 2),
        old_v.reshape(S, PR, H).transpose(1, 0, 2),
        norm_gain.reshape(2, 1, H),
        tokens,
        cotangent,
    )
    moment_next = beta_one * moment.astype(F32) + (1.0 - beta_one) * grad
    second_next = beta_two * square.astype(F32) + (1.0 - beta_two) * grad * grad
    fix_one = 1.0 - beta_one**step_count
    fix_two = 1.0 - beta_two**step_count
    direction = moment_next / fix_one / (jnp.sqrt(second_next / fix_two) + adam_eps)
    kept = master.astype(F32)
    updated = kept - learn_rate * (direction + decay_rate * kept)
    return updated[None], moment_next.astype(BF16)[None], second_next.astype(BF16)[None]


def solution(mesh):
    placed = (
        P(None, "dp", "section", None, "mp"),
        P(None, "dp", "section", None, "mp"),
        P(None, "dp", "section", None, "mp"),
        P(),
        P("section", None),
        P(None, "dp", None),
        P(None, "dp", None),
    )
    return jax.shard_map(
        local,
        mesh=mesh,
        in_specs=placed,
        out_specs=(P("section", "dp", "mp"), P("section", "dp", "mp"), P("section", "dp", "mp")),
        check_vma=False,
    )
```

```python
import functools

import jax
import jax.numpy as jnp
from jax import lax
from jax.experimental import pallas as pl
from jax.experimental.pallas import tpu as pltpu
from jax.sharding import PartitionSpec as P

eps_norm = 1e-05
beta_one = 0.9
beta_two = 0.95
learn_rate = 0.001
decay_rate = 0.1
adam_eps = 1e-08
step_count = 1000.0

MESH = pl.DeviceIdType.MESH
F32 = jnp.float32
BF16 = jnp.bfloat16
XS = 4


def remote(src, dst, send_sem, recv_sem, device):
    return pltpu.make_async_remote_copy(
        src_ref=src,
        dst_ref=dst,
        send_sem=send_sem,
        recv_sem=recv_sem,
        device_id=device,
        device_id_type=MESH,
    )


def relay_plan(rows):
    two_thirds = max(16, (rows * 2 // 3 + 15) // 16 * 16)
    half = (rows // 2 + 15) // 16 * 16
    return two_thirds, half


def feature_width(rows, half):
    return max(
        -(-(rows * k % 128 + rows) // 128) * 128 for k in range(half // rows)
    )


def kernel(
    sizes,
    slot_layer,
    old_w_hbm,
    old_m_hbm,
    old_v_hbm,
    gain,
    tokens,
    cotangent,
    grad_out,
    block_out,
    m_out,
    v_out,
    old_w,
    old_m,
    old_v,
    w_send,
    m_send,
    v_send,
    w_recv,
    m_recv,
    v_recv,
    pick,
    wide,
    block,
    first,
    second,
    weights,
    flipped,
    acts,
    outs,
    preacts,
    scales,
    normed,
    raw_feats,
    feats,
    grads_in,
    grads_out,
    dpres,
    part_send,
    part_recv,
    stat_send,
    stat_recv,
    ws,
    wr,
    ms,
    mr,
    vs,
    vr,
    gs,
    gr,
    fs,
    fr,
    rs,
    rr,
    ps,
    pr,
    ss,
    sr,
    bs,
    br,
    ts,
    tr,
    ds,
    dr,
    local_sem,
    out_sem,
    in_sem,
):
    S, D, pr_rows, H, MB, R = sizes
    RB = S * pr_rows
    TOK = MB * R
    E = 2 * H
    s = lax.axis_index("section")
    a = lax.axis_index("dp")
    c = lax.axis_index("mp")
    sib = {"mp": 1 - c}
    lanes = H // 128
    cut = (lanes + 1) // 2 * 128
    chunks = ((0, cut), (cut, H - cut))
    width = feature_width(RB, H)
    rounds = 2 if S % 2 == 0 and RB // 2 % 16 == 0 else 1
    G, GR = S // rounds, RB // rounds
    group = s // G
    spot = lax.rem(s, G)
    groups = [group, 1 - group][:rounds]
    near = sorted(range(1, G), key=lambda k: min(k, G - k))

    barrier = pltpu.get_barrier_semaphore()

    @pl.loop(1, S)
    def _(k):
        pl.semaphore_signal(
            barrier, inc=1, device_id={"section": lax.rem(s + k, S)}, device_id_type=MESH
        )

    @pl.loop(1, D)
    def _(k):
        pl.semaphore_signal(
            barrier, inc=1, device_id={"dp": lax.rem(a + k, D)}, device_id_type=MESH
        )

    pl.semaphore_signal(barrier, inc=1, device_id=sib, device_id_type=MESH)

    loads = [
        pltpu.make_async_copy(src, dst, in_sem.at[i])
        for i, (src, dst) in enumerate(
            ((old_w_hbm, old_w), (old_m_hbm, old_m), (old_v_hbm, old_v))
        )
    ]
    for load in loads:
        load.start()

    @pl.when(s == 0)
    def _():
        @pl.loop(0, MB)
        def _(b):
            pltpu.make_async_copy(
                tokens.at[b, :, pl.ds(pl.multiple_of(c * H, 128), H)],
                acts.at[b, c],
                local_sem.at[b],
            ).start()

    @pl.when(s == S - 1)
    def _():
        @pl.loop(0, MB)
        def _(b):
            pltpu.make_async_copy(
                cotangent.at[b, :, pl.ds(pl.multiple_of(c * H, 128), H)],
                grads_in.at[b],
                local_sem.at[MB + b],
            ).start()

    loads[0].wait()

    def slot_of(layer):
        slot = jnp.int32(0)
        for j in range(1, S):
            slot = jnp.where(slot_layer[j] == layer, j, slot)
        return slot

    @pl.loop(0, S)
    def _(k):
        base = slot_of(k) * (pr_rows * lanes)
        for j in range(lanes):
            w_send[k, :, 128 * j : 128 * (j + 1)] = old_w[
                pl.ds(base + j, pr_rows, stride=lanes), :
            ].astype(BF16)

    pl.semaphore_wait(barrier, S + D - 1)

    def send_piece(send, recv, send_sems, recv_sems, to):
        remote(
            send.at[to], recv.at[s], send_sems.at[to], recv_sems.at[s], {"section": to}
        ).start()

    def peers(which, offsets):
        return [groups[which] * G + lax.rem(spot + k, G) for k in offsets]

    def arrived(send, recv, send_sems, recv_sems, which):
        for of in peers(which, near if which == 0 else range(G)):
            remote(
                send.at[of], recv.at[of], send_sems.at[of], recv_sems.at[of], {"section": of}
            ).wait_recv()

    def drained(send, recv, send_sems, recv_sems):
        @pl.loop(1, S)
        def _(k):
            of = lax.rem(s + k, S)
            remote(
                send.at[of], recv.at[of], send_sems.at[of], recv_sems.at[of], {"section": of}
            ).wait_send()

    def assemble(recv, dst, which):
        base = groups[which] * G
        rows = pl.ds(pl.multiple_of(groups[which] * GR, 16), GR)

        @pl.loop(0, lanes)
        def _(j):
            cols = pl.ds(pl.multiple_of(j * 128, 128), 128)
            for i in range(G):
                wide[pr_rows * i : pr_rows * (i + 1), :] = recv[
                    base + i, 0:pr_rows, cols
                ].astype(F32)
            dst[rows, cols] = wide[...].astype(BF16)

    @pl.loop(0, S)
    def _(k):
        to = lax.rem(k, rounds) * G + k // rounds

        @pl.when(to != s)
        def _():
            send_piece(w_send, w_recv, ws, wr, to)

    w_recv[s] = w_send[s]

    def rows_of(owner, r0, n):
        return weights.at[pl.ds(pl.multiple_of(owner * RB + r0, 16), n), :]

    def prepare():
        padded = pick.shape[0] // S

        @pl.loop(0, S)
        def _(k):
            shape = (padded, pr_rows * S)
            row = lax.broadcasted_iota(jnp.int32, shape, 0)
            col = lax.broadcasted_iota(jnp.int32, shape, 1)
            hit = col == row * S + slot_of(k)
            pick[pl.ds(pl.multiple_of(k * padded, 16), padded), :] = jnp.where(
                hit & (row < pr_rows), 1.0, 0.0
            ).astype(BF16)

        def select(old, send):
            @pl.loop(0, lanes)
            def _(j):
                cols = pl.ds(pl.multiple_of(j * 128, 128), 128)
                flat = old[:, :, cols].reshape(pr_rows * S, 128)
                send[:, :, cols] = (
                    jnp.dot(pick[...], flat, preferred_element_type=F32)
                    .astype(BF16)
                    .reshape(S, padded, 128)[:, :pr_rows]
                )

        loads[1].wait()
        select(old_m, m_send)
        loads[2].wait()
        select(old_v, v_send)
        m_recv[s] = m_send[s]
        v_recv[s] = v_send[s]

    pending = []

    def begin(which):
        arrived(w_send, w_recv, ws, wr, which)
        assemble(w_recv, block, which)
        at = pl.multiple_of(groups[which] * GR, 16)
        own = pltpu.make_async_copy(
            block.at[pl.ds(at, GR), :], rows_of(a, at, GR), local_sem.at[2 * MB + which]
        )
        own.start()
        return own

    def relays(which):
        x = lax.rem(a, XS)
        h = a // XS
        base = pl.multiple_of(groups[which] * GR, 16)

        def at(dx, dh):
            hh = (1 - h) if dh else h
            return hh * XS + lax.rem(x + dx + XS, XS)

        third, half = relay_plan(GR)
        up, down, across = at(1, 0), at(-1, 0), at(0, 1)

        def start(sem, src, owner, r0, n, to):
            sem = sem + 14 * which
            cp = remote(
                src, rows_of(owner, base + r0, n), gs.at[sem], gr.at[sem], {"dp": to}
            )
            cp.start()
            pending.append(cp)

        def relay(sem, owner, r0, n, to):
            start(sem, rows_of(owner, base + r0, n), owner, r0, n, to)

        def landed(sem, owner, r0, n):
            there = rows_of(owner, base + r0, n)
            pltpu.make_async_copy(there, there, gr.at[sem + 14 * which]).wait()

        def blk(r0, n):
            return block.at[pl.ds(pl.multiple_of(base + r0, 16), n), :]

        begun = begin(which)
        start(0, blk(third, GR - third), a, third, GR - third, across)
        start(1, blk(0, third), a, 0, third, across)
        start(2, blk(0, half), a, 0, half, up)
        start(3, blk(half, GR - half), a, half, GR - half, down)
        start(4, blk(half, GR - half), a, half, GR - half, up)
        start(5, blk(0, half), a, 0, half, down)
        yield
        landed(0, across, third, GR - third)
        relay(6, across, third, GR - third, up)
        relay(7, across, third, GR - third, down)
        landed(2, down, 0, half)
        relay(8, down, 0, half, up)
        landed(3, up, half, GR - half)
        relay(9, up, half, GR - half, down)
        yield
        landed(4, down, half, GR - half)
        relay(10, down, 0, third, across)
        landed(5, up, 0, half)
        relay(11, up, 0, third, across)
        yield
        landed(1, across, 0, third)
        landed(6, at(-1, 1), third, GR - third)
        landed(10, at(-1, 1), 0, third)
        relay(12, at(-1, 1), 0, half, up)
        landed(7, at(1, 1), third, GR - third)
        landed(11, at(1, 1), 0, third)
        relay(13, at(1, 1), half, GR - half, down)
        yield
        landed(8, at(2, 0), 0, half)
        landed(9, at(2, 0), half, GR - half)
        landed(12, at(2, 1), 0, half)
        landed(13, at(2, 1), half, GR - half)
        begun.wait()
        yield

    def direct(which):
        base = pl.multiple_of(groups[which] * GR, 16)
        begun = begin(which)
        for k in range(1, D):
            to = lax.rem(a + k, D)
            sem = k + 14 * which
            cp = remote(
                block.at[pl.ds(base, GR), :],
                rows_of(a, base, GR),
                gs.at[sem],
                gr.at[sem],
                {"dp": to},
            )
            cp.start()
            pending.append(cp)
        yield
        for k in range(1, D):
            there = rows_of(lax.rem(a - k + D, D), base, GR)
            pltpu.make_async_copy(there, there, gr.at[k + 14 * which]).wait()
        begun.wait()
        for _ in range(4):
            yield

    def moments(which, offsets):
        for to in peers(which, offsets):
            send_piece(m_send, m_recv, ms, mr, to)
            send_piece(v_send, v_recv, vs, vr, to)

    routes = [(relays if D == 2 * XS else direct)(which) for which in range(rounds)]
    next(routes[0])
    prepare()
    moments(0, near)
    if rounds == 1:
        for _ in routes[0]:
            pass
    else:
        for which in (0, 0, 1, 0, 1, 1, 1, 0, 1):
            next(routes[which])

    block_copy = pltpu.make_async_copy(block, block_out, out_sem.at[0])
    block_copy.start()

    early = s < (S + 1) // 2

    def flip():
        for part_index in range(2):

            @pl.loop(0, lanes * lanes)
            def _(t):
                i = pl.multiple_of(t // lanes * 128, 128)
                j = pl.multiple_of(lax.rem(t, lanes) * 128, 128)
                flipped[part_index, pl.ds(j, 128), pl.ds(i, 128)] = jnp.transpose(
                    weights[pl.ds(pl.multiple_of(part_index * H + i, 128), 128), pl.ds(j, 128)]
                )

    behind = [0] + [k for k in near if 2 * k > G]
    ahead = [k for k in near if 2 * k <= G]
    if rounds == 2:
        moments(1, behind)

    @pl.when(jnp.logical_not(early))
    def _():
        flip()

    gain_own = gain[c]
    gain_sib = gain[1 - c]

    def w_rows(half_index, chunk):
        at, n = chunk
        return pl.ds(pl.multiple_of(half_index * H + at, 128), n)

    @pl.loop(0, MB)
    def _(b):
        total = jnp.zeros((R, H), F32)
        square = jnp.zeros((R, 1), F32)
        own, other = [], []

        @pl.when(s == 0)
        def _():
            pltpu.make_async_copy(
                tokens.at[b, :, pl.ds(pl.multiple_of(c * H, 128), H)],
                acts.at[b, c],
                local_sem.at[b],
            ).wait()

        for q, (at, n) in enumerate(chunks):
            here = acts.at[b, c, :, pl.ds(at, n)]

            @pl.when(s > 0)
            def _():
                pltpu.make_async_copy(here, here, fr.at[b, q]).wait()

            remote(here, here, rs.at[b, q], rr.at[b, q], sib).start()
            x = acts[b, c, :, at : at + n].astype(F32)
            own.append(x)
            square = square + jnp.sum(x * x, axis=1, keepdims=True)
            total = total + jnp.dot(
                (x * gain_own[:, at : at + n]).astype(BF16),
                weights[w_rows(c, (at, n)), :],
                preferred_element_type=F32,
            )
        for q, (at, n) in enumerate(chunks):
            there = acts.at[b, 1 - c, :, pl.ds(at, n)]
            pltpu.make_async_copy(there, there, rr.at[b, q]).wait()
            x = acts[b, 1 - c, :, at : at + n].astype(F32)
            other.append(x)
            square = square + jnp.sum(x * x, axis=1, keepdims=True)
            x_gain = (x * gain_sib[:, at : at + n]).astype(BF16)
            if q == 0:
                total = total + jnp.dot(
                    x_gain, weights[w_rows(1 - c, (at, n)), :], preferred_element_type=F32
                )
        scale = lax.rsqrt(square * (1.0 / E) + eps_norm)
        for t, (to_at, to_n) in enumerate(chunks):
            pre = (
                total[:, to_at : to_at + to_n]
                + jnp.dot(
                    x_gain,
                    weights[w_rows(1 - c, chunks[1]), to_at : to_at + to_n],
                    preferred_element_type=F32,
                )
            ) * scale
            outs[b, :, to_at : to_at + to_n] = (own[t] + jax.nn.silu(pre)).astype(BF16)

            @pl.when(s < S - 1)
            def _():
                remote(
                    outs.at[b, :, pl.ds(to_at, to_n)],
                    acts.at[b, c, :, pl.ds(to_at, to_n)],
                    fs.at[b, t],
                    fr.at[b, t],
                    {"section": lax.rem(s + 1, S)},
                ).start()

            preacts[b, :, to_at : to_at + to_n] = pre
        scales[b] = jnp.broadcast_to(scale, (R, 128))
        for q, (at, n) in enumerate(chunks):
            cols = slice(at, at + n)
            normed[c, b, :, cols] = (own[q] * scale * gain_own[:, cols]).astype(BF16)
            normed[1 - c, b, :, cols] = (other[q] * scale * gain_sib[:, cols]).astype(BF16)

    per_half = H // RB

    def window(owner):
        offset = lax.rem(owner, per_half) * RB
        return owner // per_half, pl.multiple_of(offset // 128 * 128, 128)

    def send_features():
        @pl.loop(1, D)
        def _(k):
            to = lax.rem(a + k, D)
            half_index, at = window(to)
            remote(
                normed.at[half_index, :, :, pl.ds(at, width)],
                raw_feats.at[:, a],
                ts.at[to],
                tr.at[a],
                {"dp": to},
            ).start()

        half_index, at = window(a)
        raw_feats[:, a] = normed[half_index, :, :, pl.ds(at, width)]

    send_features()

    def moment_rows(recv, send, send_sems, recv_sems, dst, which):
        arrived(send, recv, send_sems, recv_sems, which)
        assemble(recv, dst, which)

    def first_rows(which):
        moment_rows(m_recv, m_send, ms, mr, first, which)

    def second_rows(which):
        moment_rows(v_recv, v_send, vs, vr, second, which)

    first_copy = pltpu.make_async_copy(first, m_out, out_sem.at[1])
    second_copy = pltpu.make_async_copy(second, v_out, out_sem.at[2])

    def near_state():
        first_rows(0)
        second_rows(0)

        @pl.loop(1, D)
        def _(k):
            of = lax.rem(a + k, D)
            pltpu.make_async_copy(raw_feats.at[:, of], raw_feats.at[:, of], tr.at[of]).wait()

        @pl.loop(0, MB)
        def _(b):
            for j in range(width // 128):
                feats[b, 128 * j : 128 * (j + 1), :] = jnp.transpose(
                    raw_feats[b, :, :, 128 * j : 128 * (j + 1)].reshape(D * R, 128)
                )

    @pl.when(early)
    def _():
        flip()
        if rounds == 2:
            moments(1, ahead)
        near_state()

    def dpre_rows(owner, b):
        return dpres.at[pl.ds(pl.multiple_of((b * D + owner) * R, R), R), :]

    my_rem = pl.multiple_of(lax.rem(lax.rem(a, per_half) * RB, 128), 16)

    def weight_grad(pair):
        @pl.loop(1, D)
        def _(k):
            of = lax.rem(a + k, D)
            for b in (2 * pair, 2 * pair + 1):
                pltpu.make_async_copy(dpre_rows(of, b), dpre_rows(of, b), dr.at[b, of]).wait()

        lhs = jnp.concatenate(
            [feats[2 * pair + i, pl.ds(my_rem, RB), :] for i in range(2)], axis=1
        )
        rows = pl.ds(pl.multiple_of(pair * 2 * D * R, 2 * D * R), 2 * D * R)

        def accumulate(cols):
            value = jnp.dot(lhs, dpres[rows, cols], preferred_element_type=F32)

            @pl.when(pair == 0)
            def _():
                grad_out[:, cols] = value

            @pl.when(pair > 0)
            def _():
                grad_out[:, cols] += value

        @pl.loop(0, H // 256)
        def _(j):
            accumulate(pl.ds(pl.multiple_of(j * 256, 128), 256))

        if H % 256:
            accumulate(pl.ds(H - H % 256, H % 256))

    @pl.loop(0, MB)
    def _(b):
        @pl.when(s == S - 1)
        def _():
            pltpu.make_async_copy(
                cotangent.at[b, :, pl.ds(pl.multiple_of(c * H, 128), H)],
                grads_in.at[b],
                local_sem.at[MB + b],
            ).wait()

        def take(q, at, n):
            here = grads_in.at[b, :, pl.ds(at, n)]

            @pl.when(s < S - 1)
            def _():
                pltpu.make_async_copy(here, here, br.at[b, q]).wait()

            upstream = grads_in[b, :, at : at + n].astype(F32)
            pre = preacts[b, :, at : at + n]
            sig = jax.nn.sigmoid(pre)
            dpre = (upstream * (sig * (1.0 + pre * (1.0 - sig)))).astype(BF16)
            dpres[pl.ds(pl.multiple_of((b * D + a) * R, R), R), at : at + n] = dpre
            return upstream, pre, dpre

        @pl.when(s == 0)
        def _():
            for q, (at, n) in enumerate(chunks):
                take(q, at, n)

        @pl.when(s > 0)
        def _():
            ups = []
            stat = jnp.zeros((R, 1), F32)
            for q, (at, n) in enumerate(chunks):
                upstream, pre, dpre = take(q, at, n)
                ups.append(upstream)
                stat = stat + jnp.sum(dpre.astype(F32) * pre, axis=1, keepdims=True)
                if q == 0:
                    away = jnp.dot(
                        dpre, flipped[1 - c, at : at + n, :], preferred_element_type=F32
                    )
                    home = jnp.dot(dpre, flipped[c, at : at + n, :], preferred_element_type=F32)
            stat_send[b] = jnp.broadcast_to(stat, (R, 128))
            remote(stat_send.at[b], stat_recv.at[b], ss.at[b], sr.at[b], sib).start()
            rows = slice(chunks[1][0], H)
            for t, (at, n) in enumerate(chunks):
                part_send[b, :, at : at + n] = (
                    away[:, at : at + n]
                    + jnp.dot(
                        dpre, flipped[1 - c, rows, at : at + n], preferred_element_type=F32
                    )
                ).astype(BF16)
                remote(
                    part_send.at[b, :, pl.ds(at, n)],
                    part_recv.at[b, :, pl.ds(at, n)],
                    ps.at[b, t],
                    pr.at[b, t],
                    sib,
                ).start()
            home = home + jnp.dot(dpre, flipped[c, rows, :], preferred_element_type=F32)
            pltpu.make_async_copy(stat_send.at[b], stat_recv.at[b], sr.at[b]).wait()
            scale = scales[b][:, :1]
            shrink = scale * scale * ((stat + stat_recv[b][:, :1]) * (1.0 / E))
            for t, (at, n) in enumerate(chunks):
                cols = slice(at, at + n)
                there = part_recv.at[b, :, pl.ds(at, n)]
                pltpu.make_async_copy(there, there, pr.at[b, t]).wait()
                dnormed = home[:, cols] + part_recv[b, :, cols].astype(F32)
                back = (
                    ups[t]
                    + scale * (gain_own[:, cols] * dnormed)
                    - acts[b, c, :, cols].astype(F32) * shrink
                )
                grads_out[b, :, cols] = back.astype(BF16)
                remote(
                    grads_out.at[b, :, pl.ds(at, n)],
                    grads_in.at[b, :, pl.ds(at, n)],
                    bs.at[b, t],
                    br.at[b, t],
                    {"section": lax.rem(s + S - 1, S)},
                ).start()

        @pl.loop(1, D)
        def _(k):
            to = lax.rem(a + k, D)
            remote(
                dpre_rows(a, b), dpre_rows(a, b), ds.at[b, to], dr.at[b, a], {"dp": to}
            ).start()

        if rounds == 2:

            @pl.when(jnp.logical_not(early) & (b == 0))
            def _():
                moments(1, ahead)

        @pl.when((s == 0) & (b >= 3) & (lax.rem(b, 2) == 1))
        def _():
            weight_grad((b - 3) // 2)

        @pl.when((s == 0) & (b == MB - 4))
        def _():
            if rounds == 2:
                first_rows(1)
            first_copy.start()

        @pl.when((s == 0) & (b == MB - 2))
        def _():
            if rounds == 2:
                second_rows(1)
            second_copy.start()

    @pl.when(jnp.logical_not(early))
    def _():
        near_state()

    @pl.when(s > 0)
    def _():
        if rounds == 2:
            first_rows(1)
            second_rows(1)
        first_copy.start()
        second_copy.start()

    @pl.loop(jnp.where(s == 0, MB // 2 - 1, 0), MB // 2)
    def _(pair):
        weight_grad(pair)

    block_copy.wait()
    first_copy.wait()
    second_copy.wait()
    drained(w_send, w_recv, ws, wr)
    drained(m_send, m_recv, ms, mr)
    drained(v_send, v_recv, vs, vr)
    for cp in pending:
        cp.wait_send()

    @pl.loop(0, MB)
    def _(b):
        for q, (at, n) in enumerate(chunks):
            here = acts.at[b, c, :, pl.ds(at, n)]
            remote(here, here, rs.at[b, q], rr.at[b, q], sib).wait_send()

            @pl.when(s < S - 1)
            def _():
                out = outs.at[b, :, pl.ds(at, n)]
                remote(out, here, fs.at[b, q], fr.at[b, q], sib).wait_send()

            @pl.when(s > 0)
            def _():
                part = part_send.at[b, :, pl.ds(at, n)]
                remote(
                    part, part_recv.at[b, :, pl.ds(at, n)], ps.at[b, q], pr.at[b, q], sib
                ).wait_send()
                back = grads_out.at[b, :, pl.ds(at, n)]
                remote(
                    back, grads_in.at[b, :, pl.ds(at, n)], bs.at[b, q], br.at[b, q], sib
                ).wait_send()

        @pl.when(s > 0)
        def _():
            remote(stat_send.at[b], stat_recv.at[b], ss.at[b], sr.at[b], sib).wait_send()

        @pl.loop(1, D)
        def _(k):
            to = lax.rem(a + k, D)
            remote(
                dpre_rows(a, b), dpre_rows(a, b), ds.at[b, to], dr.at[b, a], {"dp": to}
            ).wait_send()

    @pl.loop(1, D)
    def _(k):
        to = lax.rem(a + k, D)
        half_index, at = window(to)
        remote(
            normed.at[half_index, :, :, pl.ds(at, width)],
            raw_feats.at[:, a],
            ts.at[to],
            tr.at[a],
            {"dp": to},
        ).wait_send()


def local(old_w, old_m, old_v, old_slot_layer, norm_gain, tokens, cotangent):
    S = lax.axis_size("section")
    D = lax.axis_size("dp")
    PR, H = old_w.shape[3], old_w.shape[4]
    MB, R = tokens.shape[0], tokens.shape[1]
    RB = S * PR
    TOK = MB * R
    E = 2 * H
    vmem = pl.BlockSpec(memory_space=pltpu.VMEM)
    anyspace = pl.BlockSpec(memory_space=pl.ANY)
    dma = pltpu.SemaphoreType.DMA
    padded = -(-PR // 16) * 16
    group_rows = RB // 2 if S % 2 == 0 and RB // 2 % 16 == 0 else RB
    width = feature_width(RB, H)
    grad, master, moment, square = pl.pallas_call(
        functools.partial(kernel, (S, D, PR, H, MB, R)),
        out_shape=(
            jax.ShapeDtypeStruct((RB, H), F32),
            jax.ShapeDtypeStruct((RB, H), BF16),
            jax.ShapeDtypeStruct((RB, H), BF16),
            jax.ShapeDtypeStruct((RB, H), BF16),
        ),
        in_specs=[pl.BlockSpec(memory_space=pltpu.SMEM), anyspace, anyspace, anyspace, vmem, anyspace, anyspace],
        out_specs=(vmem, anyspace, anyspace, anyspace),
        scratch_shapes=[
            pltpu.VMEM((S * PR * H // 128, 128), F32),
            pltpu.VMEM((PR, S, H), BF16),
            pltpu.VMEM((PR, S, H), BF16),
            pltpu.VMEM((S, PR, H), BF16),
            pltpu.VMEM((S, PR, H), BF16),
            pltpu.VMEM((S, PR, H), BF16),
            pltpu.VMEM((S, PR, H), BF16),
            pltpu.VMEM((S, PR, H), BF16),
            pltpu.VMEM((S, PR, H), BF16),
            pltpu.VMEM((S * padded, PR * S), BF16),
            pltpu.VMEM((group_rows, 128), F32),
            pltpu.VMEM((RB, H), BF16),
            pltpu.VMEM((RB, H), BF16),
            pltpu.VMEM((RB, H), BF16),
            pltpu.VMEM((E, H), BF16),
            pltpu.VMEM((2, H, H), BF16),
            pltpu.VMEM((MB, 2, R, H), BF16),
            pltpu.VMEM((MB, R, H), BF16),
            pltpu.VMEM((MB, R, H), F32),
            pltpu.VMEM((MB, R, 128), F32),
            pltpu.VMEM((2, MB, R, H), BF16),
            pltpu.VMEM((MB, D, R, width), BF16),
            pltpu.VMEM((MB, width, D * R), BF16),
            pltpu.VMEM((MB, R, H), BF16),
            pltpu.VMEM((MB, R, H), BF16),
            pltpu.VMEM((D * TOK, H), BF16),
            pltpu.VMEM((MB, R, H), BF16),
            pltpu.VMEM((MB, R, H), BF16),
            pltpu.VMEM((MB, R, 128), F32),
            pltpu.VMEM((MB, R, 128), F32),
            dma((S,)),
            dma((S,)),
            dma((S,)),
            dma((S,)),
            dma((S,)),
            dma((S,)),
            dma((28,)),
            dma((28,)),
            dma((MB, 2)),
            dma((MB, 2)),
            dma((MB, 2)),
            dma((MB, 2)),
            dma((MB, 2)),
            dma((MB, 2)),
            dma((MB,)),
            dma((MB,)),
            dma((MB, 2)),
            dma((MB, 2)),
            dma((D,)),
            dma((D,)),
            dma((MB, D)),
            dma((MB, D)),
            dma((2 * MB + 2,)),
            dma((3,)),
            dma((3,)),
        ],
        compiler_params=pltpu.CompilerParams(
            collective_id=0, has_side_effects=True, vmem_limit_bytes=63_000_000
        ),
    )(
        old_slot_layer,
        old_w.reshape(S * PR * H // 128, 128),
        old_m.reshape(S, PR, H).transpose(1, 0, 2),
        old_v.reshape(S, PR, H).transpose(1, 0, 2),
        norm_gain.reshape(2, 1, H),
        tokens,
        cotangent,
    )
    moment_next = beta_one * moment.astype(F32) + (1.0 - beta_one) * grad
    second_next = beta_two * square.astype(F32) + (1.0 - beta_two) * grad * grad
    fix_one = 1.0 - beta_one**step_count
    fix_two = 1.0 - beta_two**step_count
    direction = moment_next / fix_one / (jnp.sqrt(second_next / fix_two) + adam_eps)
    kept = master.astype(F32)
    updated = kept - learn_rate * (direction + decay_rate * kept)
    return updated[None], moment_next.astype(BF16)[None], second_next.astype(BF16)[None]


def solution(mesh):
    placed = (
        P(None, "dp", "section", None, "mp"),
        P(None, "dp", "section", None, "mp"),
        P(None, "dp", "section", None, "mp"),
        P(),
        P("section", None),
        P(None, "dp", None),
        P(None, "dp", None),
    )
    return jax.shard_map(
        local,
        mesh=mesh,
        in_specs=placed,
        out_specs=(P("section", "dp", "mp"), P("section", "dp", "mp"), P("section", "dp", "mp")),
        check_vma=False,
    )
```
